128 devices in a mesh: chaos: 8 (over z, core), space: 16 (over x, y).
Axes of the slice: x: 4, y: 4, z: 4, core: 2. Of those that a mesh axis runs over, the one named last changes fastest.
Arguments:
- panels: bfloat16 [216, 48, 2304], P('chaos', 'space'), may hold values from -6 to 6
- mean_field: float32 [48, 2304], P('space'), may hold values from 0.5 to 2
- fluctuations: float32 [6, 48, 2304], P(None, 'space'), may hold values from -1.5 to 1.5
- products: float32 [1218], replicated, may hold values from -4 to 4
- triples: int32 [1218, 3], replicated, may hold values from 0 to 209, as said below
- owner_slot: int32 [210], replicated, may hold values from 0 to 215, as said below
Outputs:
- first_apply: bfloat16 [216, 48, 2304], P('chaos', 'space')
- second_apply: bfloat16 [216, 48, 2304], P('chaos', 'space')
The draws below stay inside these ranges and needn't reach their ends.
Inputs may be any that keep to these rules, and one draw needn't show every extreme that they name: `triples`: each row (i, j, k) names a nonzero of G_k; i and j are below 210, k below 7; repeated rows add; every chaos coefficient is some row's i and some row's j. `owner_slot`: distinct slots; slot s belongs to the group s // 27 along chaos.
All inputs are finite; a program needn't handle non-finite values.
Results may differ from the reference program's by a relative error of at most 0.007.
Values may be sent and summed in bfloat16 or wider, within the bound.
A program may use at most 64 MiB of HBM per device.

```python
import math
import jax
import jax.numpy as jnp
from jax import lax

P_SIZE = 210
NPAR = 6
KF = 7
NNZ = 1218
NXY = 48
SLOTS = 216
NZ = 48
XY = 2304


def draw_triples(key, part):
    keys_all = jax.random.split(key, 5)
    row_index = jnp.concatenate([jax.random.permutation(keys_all[0], P_SIZE).astype(jnp.int32), jax.random.randint(keys_all[1], (NNZ - P_SIZE,), 0, P_SIZE).astype(jnp.int32)])
    column_index = jnp.concatenate([jax.random.permutation(keys_all[2], P_SIZE).astype(jnp.int32), jax.random.randint(keys_all[3], (NNZ - P_SIZE,), 0, P_SIZE).astype(jnp.int32)])
    fields = jax.random.randint(keys_all[4], (NNZ,), 0, KF).astype(jnp.int32)
    return jnp.stack([row_index, column_index, fields], axis=1).astype(jnp.int32)


def draw_owner_slot(key, part):
    keys_all = jax.random.split(key, 2)
    middle_slots = (jax.random.permutation(keys_all[0], SLOTS - 2) + 1).astype(jnp.int32)
    chosen = jnp.concatenate([jnp.array([0, SLOTS - 1], jnp.int32), middle_slots[SLOTS - P_SIZE:]])
    return jax.random.permutation(keys_all[1], chosen).astype(jnp.int32)


def block_levels(rng, dims, cuts, least, largest):
    gain, own = 1.0, jax.random.fold_in(rng, 6)
    for dim, parts in cuts:
        heights = jnp.exp(jax.random.uniform(jax.random.fold_in(own, dim), (parts,), jnp.float32, least / len(cuts), largest / len(cuts)))
        gain = gain * jnp.repeat(heights, dims[dim] // parts).reshape([-1 if axis == dim else 1 for axis in range(len(dims))])
    return gain


def gaussian(rng, shape, scale, most, shards=(), held_as=jnp.bfloat16):
    values = jax.random.normal(rng, shape, jnp.float32) * scale
    if len(shards) > 0:
        values = block_levels(rng, shape, shards, -0.22, 0.18) * values
    return jnp.clip(values, min=-most, max=most).astype(held_as)


def setup_inputs(seed: int = 0) -> dict:
    key_list = jax.random.split(jax.random.key(seed), 7)
    panels = gaussian(key_list[0], (SLOTS, NZ, XY), 1.0, 6.0, ((0, 8), (1, 16)))
    mean_field = jnp.clip(jnp.exp(math.log(2.0) - 1.3862944 * jax.random.uniform(key_list[1], (NZ, XY), jnp.float32) ** block_levels(key_list[1], (NZ, XY), ((0, 16),), -0.2, 0.2)), 0.5, 2.0)
    fluctuations = gaussian(key_list[2], (NPAR, NZ, XY), 0.3, 1.5, ((1, 16),), jnp.float32)
    products = gaussian(key_list[3], (NNZ,), 1.0, 4.0, (), jnp.float32)
    triples = draw_triples(jax.random.fold_in(key_list[6], 71), 0)
    owner_slot = draw_owner_slot(jax.random.fold_in(key_list[6], 71), 0)
    return dict(panels=panels, mean_field=mean_field, fluctuations=fluctuations, products=products, triples=triples, owner_slot=owner_slot)


scale_factor = 0.15


def shifted(source, offset, inside):
    length_last = source.shape[-1]
    padding = [(0, 0)] * (source.ndim - 1)
    if offset > 0:
        moved_values = jnp.pad(source[..., offset:], padding + [(0, offset)])
    else:
        moved_values = jnp.pad(source[..., :length_last + offset], padding + [(-offset, 0)])
    return jnp.where(inside, moved_values, jnp.zeros_like(moved_values))


def diffusion(extended, conductance_ext, side_cells):
    center = extended[..., 1:-1, :]
    conduct = conductance_ext[1:-1]
    flux_sum = 0.5 * (conduct + conductance_ext[2:]) * (center - extended[..., 2:, :])
    flux_sum = flux_sum + 0.5 * (conduct + conductance_ext[:-2]) * (center - extended[..., :-2, :])
    column = lax.iota(jnp.int32, center.shape[-1]) % side_cells
    everywhere = column >= 0
    for offset, inside in ((1, column < side_cells - 1), (-1, column > 0), (side_cells, everywhere), (-side_cells, everywhere)):
        flux_sum = flux_sum + 0.5 * (conduct + shifted(conduct, offset, inside)) * (center - shifted(center, offset, inside))
    return flux_sum


def first_rows(triples):
    entry_keys = (triples[:, 2] * P_SIZE + triples[:, 0]) * P_SIZE + triples[:, 1]
    matching = entry_keys[:, None] == entry_keys[None, :]
    earlier = lax.iota(jnp.int32, NNZ)[None, :] < lax.iota(jnp.int32, NNZ)[:, None]
    return jnp.logical_not(jnp.any(matching & earlier, axis=1))


def galerkin_apply(chaos_panels, padded_coef, tables, triples, leading):
    flat_panels = chaos_panels.reshape(P_SIZE, NZ * XY)
    result = jnp.zeros((P_SIZE, NZ, XY), jnp.float32)
    entry_values = tables[triples[:, 2], triples[:, 0], triples[:, 1]].astype(jnp.float32)
    for field_index in range(KF):
        weights = jnp.where(leading & (triples[:, 2] == field_index), entry_values, jnp.zeros_like(entry_values))

        def add_entry(running, entry):
            weight, row_index, column_index = entry
            return running.at[row_index].add(weight * flat_panels[column_index].astype(jnp.float32)), None

        running, _ = lax.scan(add_entry, jnp.zeros((P_SIZE, NZ * XY), jnp.float32), (weights, triples[:, 0], triples[:, 1]))
        combined = lax.optimization_barrier(running.astype(jnp.bfloat16))
        combined = combined.astype(jnp.float32).reshape(P_SIZE, NZ, XY)
        extended = jnp.pad(combined, ((0, 0), (1, 1), (0, 0)))
        result = result + diffusion(extended, padded_coef[field_index], NXY)
    return (scale_factor * result).astype(jnp.bfloat16)


def reference(panels, mean_field, fluctuations, products, triples, owner_slot):
    coefficients = jnp.concatenate([mean_field[None], fluctuations], axis=0)
    padded_coef = jnp.pad(coefficients, ((0, 0), (1, 1), (0, 0)))
    tables = jnp.zeros((KF, P_SIZE, P_SIZE), jnp.float32).at[triples[:, 2], triples[:, 0], triples[:, 1]].add(products)
    tables = tables.astype(jnp.bfloat16)
    leading = first_rows(triples)
    chaos_panels = panels[owner_slot]
    first_values = galerkin_apply(chaos_panels, padded_coef, tables, triples, leading)
    second_values = galerkin_apply(first_values, padded_coef, tables, triples, leading)
    empty_slots = jnp.zeros((SLOTS, NZ, XY), jnp.bfloat16)
    return empty_slots.at[owner_slot].set(first_values), empty_slots.at[owner_slot].set(second_values)
```

```python
import functools

import jax
import jax.numpy as jnp
from jax import lax
from jax.experimental import pallas as pl
from jax.experimental.pallas import tpu as pltpu
from jax.sharding import PartitionSpec as P

MESH = pl.DeviceIdType.MESH
SIDE = 48
CELLS = 288
WIN = 384
PAD = 32
HALF = 0.5 * 0.15


def tile_window(part):
    start = CELLS * part - SIDE
    return start // 128, start % 128


def kernel(
    groups, slabs, fields, nnz,
    panel_ref, coef_ref, row_ref, col_ref, val_ref,
    first_ref, second_ref,
    send_buf, x1, x2, y1, y2, halo_low, halo_high, land1, land2,
    coef_low, coef_high, weight, onehot_rows, onehot_cols, table, scaled,
    a2a_send, a2a_recv, self_sem, z_send, z_recv, c_send, c_recv,
    h_send, h_recv, o1_send, o1_recv, o2_send, o2_recv, z2_send, z2_recv,
):
    part = lax.axis_index("chaos")
    slab = lax.axis_index("space")
    own_rows = panel_ref.shape[1]
    has_low, has_high = slab > 0, slab < slabs - 1
    left, right = part > 0, part < groups - 1
    bf16, f32 = jnp.bfloat16, jnp.float32

    barrier = pltpu.get_barrier_semaphore()
    for step in range(1, groups):
        peer = lax.rem(part + step, groups)
        pl.semaphore_signal(barrier, inc=1, device_id=(peer, slab), device_id_type=MESH)

    @pl.when(has_low)
    def _():
        pl.semaphore_signal(barrier, inc=1, device_id=(part, slab - 1), device_id_type=MESH)

    @pl.when(has_high)
    def _():
        pl.semaphore_signal(barrier, inc=1, device_id=(part, slab + 1), device_id_type=MESH)

    lane = lax.broadcasted_iota(jnp.int32, (1, WIN), 1)
    send_buf[...] = jnp.zeros_like(send_buf)
    for target in range(groups):
        tile, offset = tile_window(target)
        first, last = max(tile, 0), min(tile + 4, 18)
        for plane in range(3):
            block = panel_ref[plane, :, first * 128 : last * 128].astype(f32)
            if tile < 0:
                block = jnp.where(lane >= SIDE, pltpu.roll(block, SIDE, 1), 0.0)
            elif last - first == 3:
                block = jnp.where(lane < WIN - SIDE, pltpu.roll(block, WIN - offset, 1), 0.0)
            else:
                block = pltpu.roll(block, 512 - offset, 1)[:, :WIN]
            send_buf[target, plane, 0:own_rows, :] = block.astype(bf16)

    pl.semaphore_wait(barrier, groups - 1 + has_low.astype(jnp.int32) + has_high.astype(jnp.int32))

    def rows_of(group):
        return pl.ds(pl.multiple_of(group * PAD, PAD), PAD)

    def a2a(peer, source):
        return pltpu.make_async_remote_copy(
            src_ref=send_buf.at[peer],
            dst_ref=x1.at[pl.ds(1, 3), rows_of(source), :],
            send_sem=a2a_send.at[peer],
            recv_sem=a2a_recv.at[source],
            device_id=(peer, slab),
            device_id_type=MESH,
        )

    for step in range(1, groups):
        a2a(lax.rem(part + step, groups), part).start()
    own = pltpu.make_async_copy(send_buf.at[part], x1.at[pl.ds(1, 3), rows_of(part), :], self_sem)
    own.start()

    def to_slab(source, target, sems, index, other):
        return pltpu.make_async_remote_copy(
            src_ref=source, dst_ref=target, send_sem=sems[0].at[index], recv_sem=sems[1].at[index],
            device_id=(part, other), device_id_type=MESH,
        )

    def low_copy(source, target, sems):
        return to_slab(source, target, sems, 0, slab - 1)

    def high_copy(source, target, sems):
        return to_slab(source, target, sems, 1, slab + 1)

    c_sems, z_sems, z2_sems = (c_send, c_recv), (z_send, z_recv), (z2_send, z2_recv)

    def start_planes(low, high):
        pl.when(has_low)(lambda: low().start())
        pl.when(has_high)(lambda: high().start())

    def finish_planes(low, high):
        @pl.when(has_low)
        def _():
            low().wait_send()
            high().wait_recv()

        @pl.when(has_high)
        def _():
            high().wait_send()
            low().wait_recv()

    @pl.when(jnp.logical_not(has_low))
    def _():
        coef_low[...] = jnp.zeros_like(coef_low)

    @pl.when(jnp.logical_not(has_high))
    def _():
        coef_high[...] = jnp.zeros_like(coef_high)

    return_low = lambda: low_copy(coef_ref.at[0], coef_high, c_sems)
    return_high = lambda: high_copy(coef_ref.at[2], coef_low, c_sems)
    start_planes(return_low, return_high)

    entries = row_ref.shape[1]
    value = val_ref[...]
    top = value.astype(bf16).astype(f32)
    middle = (value - top).astype(bf16).astype(f32)
    bottom = value - top - middle

    @pl.loop(0, 16)
    def _(block):
        index = lax.broadcasted_iota(jnp.int32, (16, entries), 0) + block * 16
        hit = row_ref[...] == index
        for piece, part_value in enumerate((top, middle, bottom)):
            at = pl.ds(pl.multiple_of(piece * 256 + block * 16, 16), 16)
            onehot_rows[at, :] = jnp.where(hit, part_value, 0.0).astype(bf16)

    @pl.loop(0, fields)
    def _(field):
        @pl.loop(0, 16)
        def _(block):
            index = lax.broadcasted_iota(jnp.int32, (16, entries), 0) + (field * 256 + block * 16)
            at = pl.ds(pl.multiple_of(block * 16, 16), 16)
            onehot_cols[at, :] = jnp.where(col_ref[...] == index, 1.0, 0.0).astype(bf16)

        pieces = lax.dot_general(
            onehot_rows[...], onehot_cols[...], (((1,), (1,)), ((), ())), preferred_element_type=f32
        )
        table[:, pl.ds(pl.multiple_of(field * 256, 256), 256)] = (
            pieces[0:256] + pieces[256:512] + pieces[512:768]
        ).astype(bf16)

    finish_planes(return_low, return_high)

    cell = lax.rem(lane, SIDE)
    inside_up, inside_down = cell < SIDE - 1, cell > 0
    for plane in range(3):
        here = coef_ref[plane]
        below = coef_low[...] if plane == 0 else coef_ref[plane - 1]
        above = coef_high[...] if plane == 2 else coef_ref[plane + 1]
        sides = (
            jnp.where(inside_up, pltpu.roll(here, WIN - 1, 1), 0.0),
            jnp.where(inside_down, pltpu.roll(here, 1, 1), 0.0),
            pltpu.roll(here, WIN - SIDE, 1),
            pltpu.roll(here, SIDE, 1),
            above,
            below,
        )
        for face, side in enumerate(sides):
            half = HALF * (here + side)
            for field in range(fields):
                weight[plane, field, face] = jnp.broadcast_to(half[field : field + 1], (8, WIN))

    def apply(x, y):
        @pl.loop(0, 3)
        def _(plane):
            @pl.loop(0, 16)
            def _(block):
                at = pl.ds(pl.multiple_of(block * 16, 16), 16)
                here = x[plane + 1, at, :].astype(f32)
                sides = (
                    jnp.where(inside_up, pltpu.roll(here, WIN - 1, 1), 0.0),
                    jnp.where(inside_down, pltpu.roll(here, 1, 1), 0.0),
                    pltpu.roll(here, WIN - SIDE, 1),
                    pltpu.roll(here, SIDE, 1),
                    x[plane + 2, at, :].astype(f32),
                    x[plane, at, :].astype(f32),
                )
                drops = [(here - side).reshape(2, 8, WIN) for side in sides]
                for field in range(fields):
                    flux = weight[plane, field, 0] * drops[0]
                    for face in range(1, 6):
                        flux = flux + weight[plane, field, face] * drops[face]
                    to = pl.ds(pl.multiple_of(field * 256 + block * 16, 16), 16)
                    scaled[to, :] = flux.reshape(16, WIN).astype(bf16)

            y[plane] = jnp.dot(table[...], scaled[...], preferred_element_type=f32).astype(bf16)

    for group in range(groups):
        @pl.when(group != part)
        def _():
            a2a(group, part).wait_send()
            a2a(part, group).wait_recv()
    own.wait()

    def clear_ends(x):
        @pl.when(jnp.logical_not(has_low))
        def _():
            x[0] = jnp.zeros(x.shape[1:], x.dtype)

        @pl.when(jnp.logical_not(has_high))
        def _():
            x[4] = jnp.zeros(x.shape[1:], x.dtype)

    clear_ends(x1)
    planes_low = lambda: low_copy(x1.at[1], x1.at[4], z_sems)
    planes_high = lambda: high_copy(x1.at[3], x1.at[0], z_sems)
    start_planes(planes_low, planes_high)
    finish_planes(planes_low, planes_high)

    apply(x1, y1)

    clear_ends(x2)
    next_low = lambda: low_copy(y1.at[0], x2.at[4], z2_sems)
    next_high = lambda: high_copy(y1.at[2], x2.at[0], z2_sems)
    start_planes(next_low, next_high)

    def row_copy(lanes, target, index, other):
        return pltpu.make_async_remote_copy(
            src_ref=y1.at[:, :, lanes], dst_ref=target, send_sem=h_send.at[index],
            recv_sem=h_recv.at[index], device_id=(other, slab), device_id_type=MESH,
        )

    rows_left = lambda: row_copy(pl.ds(0, 128), halo_high, 0, part - 1)
    rows_right = lambda: row_copy(pl.ds(256, 128), halo_low, 1, part + 1)
    pl.when(left)(lambda: rows_left().start())
    pl.when(right)(lambda: rows_right().start())

    def out_copy(y, land, peer, source, sems):
        return pltpu.make_async_remote_copy(
            src_ref=y.at[:, rows_of(peer), :], dst_ref=land.at[source],
            send_sem=sems[0].at[peer], recv_sem=sems[1].at[source],
            device_id=(peer, slab), device_id_type=MESH,
        )

    def start_out(y, land, sems):
        for step in range(1, groups):
            out_copy(y, land, lax.rem(part + step, groups), part, sems).start()

    def finish_out(y, land, sems):
        for group in range(groups):
            @pl.when(group != part)
            def _():
                out_copy(y, land, group, part, sems).wait_send()
                out_copy(y, land, part, group, sems).wait_recv()

    o1_sems, o2_sems = (o1_send, o1_recv), (o2_send, o2_recv)
    start_out(y1, land1, o1_sems)
    own1 = pltpu.make_async_copy(y1.at[:, rows_of(part), :], land1.at[part], self_sem)
    own1.start()

    @pl.when(left)
    def _():
        rows_left().wait_send()
        rows_right().wait_recv()

    @pl.when(right)
    def _():
        rows_right().wait_send()
        rows_left().wait_recv()

    @pl.when(jnp.logical_not(left))
    def _():
        halo_low[...] = jnp.zeros_like(halo_low)

    @pl.when(jnp.logical_not(right))
    def _():
        halo_high[...] = jnp.zeros_like(halo_high)

    tile_lane = lax.broadcasted_iota(jnp.int32, (1, 128), 1)

    @pl.loop(0, 3)
    def _(plane):
        @pl.loop(0, 8)
        def _(block):
            at = pl.ds(pl.multiple_of(block * 32, 32), 32)
            low = pltpu.roll(halo_low[plane, at, :].astype(f32), 96, 1)
            high = pltpu.roll(halo_high[plane, at, :].astype(f32), 32, 1)
            x2[plane + 1, at, 0:128] = jnp.where(
                tile_lane < 48, low, y1[plane, at, 0:128].astype(f32)
            ).astype(bf16)
            x2[plane + 1, at, 128:256] = y1[plane, at, 128:256]
            x2[plane + 1, at, 256:384] = jnp.where(
                tile_lane >= 80, high, y1[plane, at, 256:384].astype(f32)
            ).astype(bf16)

    finish_planes(next_low, next_high)
    apply(x2, y2)

    start_out(y2, land2, o2_sems)
    own1.wait()
    own2 = pltpu.make_async_copy(y2.at[:, rows_of(part), :], land2.at[part], self_sem)
    own2.start()

    def assemble(land, out_ref):
        for plane in range(3):
            carry = None
            for source in range(groups):
                tile, offset = divmod(CELLS * source, 128)
                block = land[source, plane, 0:own_rows, :].astype(f32)
                block = pltpu.roll(block, (offset - SIDE) % WIN, 1)
                head = block[:, 0:128]
                if offset:
                    head = jnp.where(tile_lane < offset, carry, head)
                out_ref[plane, :, tile * 128 : tile * 128 + 128] = head.astype(bf16)
                out_ref[plane, :, tile * 128 + 128 : tile * 128 + 256] = block[:, 128:256].astype(bf16)
                carry = block[:, 256:384]
                if offset + CELLS == WIN:
                    out_ref[plane, :, tile * 128 + 256 : tile * 128 + 384] = carry.astype(bf16)

    finish_out(y1, land1, o1_sems)
    assemble(land1, first_ref)
    own2.wait()
    finish_out(y2, land2, o2_sems)
    assemble(land2, second_ref)


def shards(groups, slabs, panels, mean_field, fluctuations, products, triples, owner_slot):
    own_rows, planes, plane_cells = panels.shape
    fields, nnz = 1 + fluctuations.shape[0], products.shape[0]
    entries = -(-nnz // 128) * 128
    part = lax.axis_index("chaos")
    panel_planes = jnp.transpose(panels, (1, 0, 2))
    coef = jnp.concatenate([mean_field[None], fluctuations], axis=0)
    coef = jnp.pad(coef, ((0, 1), (0, 0), (SIDE, SIDE)))
    coef = lax.dynamic_slice_in_dim(coef, part * CELLS, WIN, axis=2)
    coef = jnp.transpose(coef, (1, 0, 2))
    padded_slot = owner_slot + (PAD - own_rows) * (owner_slot // own_rows)
    names = lax.iota(jnp.int32, owner_slot.shape[0])

    def slots(indices):
        return jnp.sum(jnp.where(indices[:, None] == names[None, :], padded_slot[None, :], 0), axis=1)

    row = jnp.pad(slots(triples[:, 0]), (0, entries - nnz))[None]
    col = jnp.pad(slots(triples[:, 1]) + 256 * triples[:, 2], (0, entries - nnz))[None]
    val = jnp.pad(products, (0, entries - nnz))[None]

    vmem = pl.BlockSpec(memory_space=pltpu.VMEM)
    out = jax.ShapeDtypeStruct(panel_planes.shape, jnp.bfloat16)
    bf16, f32 = jnp.bfloat16, jnp.float32
    dma = pltpu.SemaphoreType.DMA
    first, second = pl.pallas_call(
        functools.partial(kernel, groups, slabs, fields, nnz),
        out_shape=(out, out),
        in_specs=[vmem] * 5,
        out_specs=(vmem, vmem),
        scratch_shapes=[
            pltpu.VMEM((groups, 3, PAD, WIN), bf16),
            pltpu.VMEM((5, 256, WIN), bf16),
            pltpu.VMEM((5, 256, WIN), bf16),
            pltpu.VMEM((3, 256, WIN), bf16),
            pltpu.VMEM((3, 256, WIN), bf16),
            pltpu.VMEM((3, 256, 128), bf16),
            pltpu.VMEM((3, 256, 128), bf16),
            pltpu.VMEM((groups, 3, PAD, WIN), bf16),
            pltpu.VMEM((groups, 3, PAD, WIN), bf16),
            pltpu.VMEM((8, WIN), f32),
            pltpu.VMEM((8, WIN), f32),
            pltpu.VMEM((3, fields, 6, 8, WIN), f32),
            pltpu.VMEM((768, entries), bf16),
            pltpu.VMEM((256, entries), bf16),
            pltpu.VMEM((256, fields * 256), bf16),
            pltpu.VMEM((fields * 256, WIN), bf16),
            dma((groups,)), dma((groups,)), dma,
            dma((2,)), dma((2,)), dma((2,)), dma((2,)), dma((2,)), dma((2,)),
            dma((groups,)), dma((groups,)), dma((groups,)), dma((groups,)),
            dma((2,)), dma((2,)),
        ],
        compiler_params=pltpu.CompilerParams(
            collective_id=0, has_side_effects=True, vmem_limit_bytes=48 * 1024 * 1024
        ),
    )(panel_planes, coef, row, col, val)
    return jnp.transpose(first, (1, 0, 2)), jnp.transpose(second, (1, 0, 2))


def solution(mesh):
    in_specs = (P("chaos", "space", None), P("space", None), P(None, "space", None), P(), P(), P())
    out_specs = (P("chaos", "space", None), P("chaos", "space", None))
    body = functools.partial(shards, mesh.shape["chaos"], mesh.shape["space"])
    return jax.shard_map(body, mesh=mesh, in_specs=in_specs, out_specs=out_specs, check_vma=False)
```

```python
import functools

import jax
import jax.numpy as jnp
from jax import lax
from jax.experimental import pallas as pl
from jax.experimental.pallas import tpu as pltpu
from jax.sharding import PartitionSpec as P

MESH = pl.DeviceIdType.MESH
SIDE = 48
CELLS = 288
WIN = 384
FLAT = 896
PAD = 32
ROWS = 256
HALF = 0.5 * 0.15
CALC = jnp.bfloat16

ORDER = ((0, 0), (0, 1), (2, 0), (2, 1), (1, 0), (1, 1), (3, 0), (3, 1))


def tile_window(part):
    start = CELLS * part - SIDE
    return start // 128, start % 128


def linear_window(ref, index, part, lane):
    tile, offset = tile_window(part)
    first, last = max(tile, 0), min(tile + 4, 18)
    block = ref[index + (slice(first * 128, last * 128),)].astype(jnp.float32)
    if tile < 0:
        return jnp.where(lane >= SIDE, pltpu.roll(block, SIDE, 1), 0.0)
    if last - first == 3:
        return jnp.where(lane < WIN - SIDE, pltpu.roll(block, WIN - offset, 1), 0.0)
    return pltpu.roll(block, 512 - offset, 1)[:, :WIN]


def flatten(planes, tile_lane):
    a, b, c = planes
    return jnp.concatenate(
        [
            a[:, 0:256],
            jnp.where(tile_lane < 32, a[:, 256:384], b[:, 0:128]),
            b[:, 128:256],
            jnp.where(tile_lane < 64, b[:, 256:384], c[:, 0:128]),
            c[:, 128:384],
        ],
        axis=1,
    )


def kernel(
    groups, slabs, fields, nnz,
    panel_ref, mean_ref, fluct_ref, triple_ref, product_ref, slot_ref,
    first_ref, second_ref,
    send_buf, x1, x2, y1, y2, edge_low, edge_high, halo_low, halo_high, land1, land2,
    coef, coef_low, coef_high, weight, drops, onehot_rows, onehot_cols, table, scaled,
    a2a_send, a2a_recv, self_sem, z_send, z_recv, c_send, c_recv,
    h_send, h_recv, o1_send, o1_recv, o2_send, o2_recv, z2_send, z2_recv,
):
    part = lax.axis_index("chaos")
    slab = lax.axis_index("space")
    own_rows = panel_ref.shape[1]
    has_low, has_high = slab > 0, slab < slabs - 1
    left, right = part > 0, part < groups - 1
    bf16, f32 = jnp.bfloat16, jnp.float32
    chip, core = part // 2, lax.rem(part, 2)

    def group_of(step):
        far, other = ORDER[step]
        return lax.rem(chip + far, groups // 2) * 2 + lax.rem(core + other, 2)

    barrier = pltpu.get_barrier_semaphore()
    for step in range(1, groups):
        pl.semaphore_signal(barrier, inc=1, device_id=(group_of(step), slab), device_id_type=MESH)

    @pl.when(has_low)
    def _():
        pl.semaphore_signal(barrier, inc=1, device_id=(part, slab - 1), device_id_type=MESH)

    @pl.when(has_high)
    def _():
        pl.semaphore_signal(barrier, inc=1, device_id=(part, slab + 1), device_id_type=MESH)

    lane = lax.broadcasted_iota(jnp.int32, (1, WIN), 1)
    tile_lane = lax.broadcasted_iota(jnp.int32, (1, 128), 1)
    send_buf[:, :, 16:32, :] = jnp.zeros((groups, 3, 16, WIN), bf16)
    for target in range(groups):
        for plane in range(3):
            block = linear_window(panel_ref, (plane, slice(None)), target, lane)
            block = pltpu.roll(block, (32 * plane - SIDE) % WIN, 1)
            send_buf[target, plane, 0:own_rows, :] = block.astype(bf16)

    coef[...] = jnp.zeros_like(coef)
    for target in range(groups):
        @pl.when(part == target)
        def _():
            for plane in range(3):
                coef[plane, 0:1, :] = linear_window(mean_ref, (slice(plane, plane + 1),), target, lane)
                for field in range(1, fields):
                    coef[plane, field : field + 1, :] = linear_window(
                        fluct_ref, (field - 1, slice(plane, plane + 1)), target, lane
                    )

    pl.semaphore_wait(barrier, groups - 1 + has_low.astype(jnp.int32) + has_high.astype(jnp.int32))

    def rows_of(group):
        return pl.ds(pl.multiple_of(group * PAD, PAD), PAD)

    def a2a(peer, source):
        return pltpu.make_async_remote_copy(
            src_ref=send_buf.at[peer],
            dst_ref=x1.at[pl.ds(1, 3), rows_of(source), :],
            send_sem=a2a_send.at[peer],
            recv_sem=a2a_recv.at[source],
            device_id=(peer, slab),
            device_id_type=MESH,
        )

    own = pltpu.make_async_copy(send_buf.at[part], x1.at[pl.ds(1, 3), rows_of(part), :], self_sem)
    own.start()
    for step in (2, 3, 4, 5, 6, 7, 1):
        a2a(group_of(step), part).start()

    def to_slab(source, target, sems, index, other):
        return pltpu.make_async_remote_copy(
            src_ref=source, dst_ref=target, send_sem=sems[0].at[index], recv_sem=sems[1].at[index],
            device_id=(part, other), device_id_type=MESH,
        )

    def start_planes(low, high):
        pl.when(has_low)(lambda: low().start())
        pl.when(has_high)(lambda: high().start())

    def arrive_planes(low, high):
        pl.when(has_low)(lambda: high().wait_recv())
        pl.when(has_high)(lambda: low().wait_recv())

    def leave_planes(low, high):
        pl.when(has_low)(lambda: low().wait_send())
        pl.when(has_high)(lambda: high().wait_send())

    @pl.when(jnp.logical_not(has_low))
    def _():
        coef_low[...] = jnp.zeros_like(coef_low)
        x1[0] = jnp.zeros(x1.shape[1:], x1.dtype)
        x2[0] = jnp.zeros(x2.shape[1:], x2.dtype)

    @pl.when(jnp.logical_not(has_high))
    def _():
        coef_high[...] = jnp.zeros_like(coef_high)
        x1[4] = jnp.zeros(x1.shape[1:], x1.dtype)
        x2[4] = jnp.zeros(x2.shape[1:], x2.dtype)

    @pl.when(jnp.logical_not(left))
    def _():
        halo_low[...] = jnp.zeros_like(halo_low)

    @pl.when(jnp.logical_not(right))
    def _():
        halo_high[...] = jnp.zeros_like(halo_high)

    c_sems, z_sems, z2_sems = (c_send, c_recv), (z_send, z_recv), (z2_send, z2_recv)
    coef_copies = (
        lambda: to_slab(coef.at[0], coef_high, c_sems, 0, slab - 1),
        lambda: to_slab(coef.at[2], coef_low, c_sems, 1, slab + 1),
    )
    start_planes(*coef_copies)

    def x_planes(group):
        rows = rows_of(group)
        return (
            lambda: to_slab(x1.at[1, rows, :], x1.at[4, rows, :], z_sems, group, slab - 1),
            lambda: to_slab(x1.at[3, rows, :], x1.at[0, rows, :], z_sems, groups + group, slab + 1),
        )

    def y_planes(group):
        rows = rows_of(group)
        return (
            lambda: to_slab(y1.at[rows, pl.ds(0, WIN)], x2.at[4, rows, :], z2_sems, group, slab - 1),
            lambda: to_slab(
                y1.at[rows, pl.ds(FLAT - WIN, WIN)], x2.at[0, rows, :], z2_sems, groups + group, slab + 1
            ),
        )

    own.wait()
    start_planes(*x_planes(part))

    slot = slot_ref[...]
    slot = slot + (PAD - own_rows) * (slot // own_rows)
    name = lax.broadcasted_iota(jnp.int32, slot.shape, 0)

    def slots(index):
        hit = name == triple_ref[index : index + 1, :]
        return jnp.sum(jnp.where(hit, slot, 0), axis=0, keepdims=True)

    row = slots(0)
    column = slots(1) + ROWS * triple_ref[2:3, :]
    value = product_ref[...]
    top = value.astype(bf16).astype(f32)
    middle = (value - top).astype(bf16).astype(f32)
    bottom = value - top - middle
    last_tile = slice(nnz // 128 * 128, nnz // 128 * 128 + 128)
    onehot_rows[:, last_tile] = jnp.zeros((3 * ROWS, 128), bf16)
    onehot_cols[:, last_tile] = jnp.zeros((ROWS, 128), bf16)

    @pl.loop(0, 16)
    def _(block):
        hit = row == lax.broadcasted_iota(jnp.int32, (16, nnz), 0) + block * 16
        for piece, part_value in enumerate((top, middle, bottom)):
            at = pl.ds(pl.multiple_of(piece * ROWS + block * 16, 16), 16)
            onehot_rows[at, 0:nnz] = jnp.where(hit, part_value, 0.0).astype(bf16)

    @pl.loop(0, fields)
    def _(field):
        @pl.loop(0, 16)
        def _(block):
            index = lax.broadcasted_iota(jnp.int32, (16, nnz), 0) + (field * ROWS + block * 16)
            at = pl.ds(pl.multiple_of(block * 16, 16), 16)
            onehot_cols[at, 0:nnz] = jnp.where(column == index, 1.0, 0.0).astype(bf16)

        pieces = lax.dot_general(
            onehot_rows[...], onehot_cols[...], (((1,), (1,)), ((), ())), preferred_element_type=f32
        )
        table[:, pl.ds(pl.multiple_of(field * ROWS, ROWS), ROWS)] = (
            pieces[0:256] + pieces[256:512] + pieces[512:768]
        ).astype(bf16)

    arrive_planes(*coef_copies)
    inside = []
    for plane in range(3):
        cell = lax.rem(lane + (WIN - 32 * plane), SIDE)
        inside.append((cell < SIDE - 1, cell > 0))

    def neighbours(here, plane, above, below):
        up, down = inside[plane]
        return (
            jnp.where(up, pltpu.roll(here, WIN - 1, 1), 0.0),
            jnp.where(down, pltpu.roll(here, 1, 1), 0.0),
            pltpu.roll(here, WIN - SIDE, 1),
            pltpu.roll(here, SIDE, 1),
            above,
            below,
        )

    halves = []
    for plane in range(3):
        turn = lambda block: pltpu.roll(block, (32 * plane - SIDE) % WIN, 1)
        here = turn(coef[plane])
        below = turn(coef_low[...] if plane == 0 else coef[plane - 1])
        above = turn(coef_high[...] if plane == 2 else coef[plane + 1])
        halves.append([HALF * (here + side) for side in neighbours(here, plane, above, below)])
    for face in range(6):
        half = flatten([halves[plane][face] for plane in range(3)], tile_lane)
        for field in range(fields):
            weight[field, face] = jnp.broadcast_to(half[field : field + 1], (16, FLAT)).astype(CALC)

    def scale(x, start):
        at = pl.ds(pl.multiple_of(start, 16), 16)
        own_planes = [x[plane + 1, at, :].astype(f32) for plane in range(3)]
        faces = []
        for plane in range(3):
            here = own_planes[plane]
            if plane == 2:
                above = pltpu.roll(x[4, at, :].astype(f32), 64, 1)
            else:
                above = pltpu.roll(own_planes[plane + 1], WIN - 32, 1)
            if plane == 0:
                below = pltpu.roll(x[0, at, :].astype(f32), WIN - 64, 1)
            else:
                below = pltpu.roll(own_planes[plane - 1], 32, 1)
            faces.append([here - side for side in neighbours(here, plane, above, below)])
        for face in range(6):
            drops[face] = flatten([faces[plane][face] for plane in range(3)], tile_lane).astype(CALC)
        for first in range(0, FLAT, 256):
            lanes = slice(first, min(first + 256, FLAT))
            drop = [drops[face, :, lanes] for face in range(6)]
            for field in range(fields):
                terms = [weight[field, face, :, lanes] * drop[face] for face in range(6)]
                flux = (terms[0] + terms[1]) + (terms[2] + terms[3]) + (terms[4] + terms[5])
                to = pl.ds(pl.multiple_of(field * ROWS + start, 16), 16)
                scaled[to, lanes] = flux.astype(bf16)

    def scale_group(x, group):
        @pl.loop(0, PAD // 16)
        def _(block):
            scale(x, group * PAD + block * 16)

    def combine(y):
        for first in range(0, FLAT, 256):
            lanes = slice(first, min(first + 256, FLAT))
            y[:, lanes] = jnp.dot(table[...], scaled[:, lanes], preferred_element_type=f32).astype(bf16)

    for step in range(1, groups):
        group = group_of(step)
        a2a(part, group).wait_recv()
        start_planes(*x_planes(group))
    for step in range(groups):
        group = group_of(step)
        arrive_planes(*x_planes(group))
        scale_group(x1, group)
    combine(y1)

    for step in range(groups):
        start_planes(*y_planes(group_of(step)))

    @pl.loop(0, 16)
    def _(block):
        at = pl.ds(pl.multiple_of(block * 16, 16), 16)
        tile = [y1[at, t * 128 : t * 128 + 128].astype(f32) for t in range(7)]
        up = [pltpu.roll(tile[t], 32, 1) for t in (0, 4, 2)]
        edge_high[at, 0:128] = jnp.where((tile_lane >= 32) & (tile_lane < 80), up[0], up[1]).astype(bf16)
        edge_high[at, 128:256] = up[2].astype(bf16)
        down = [pltpu.roll(tile[t], 96, 1) for t in (1, 2, 6, 4)]
        edge_low[at, 0:128] = jnp.where(
            tile_lane >= 96, down[1], jnp.where(tile_lane >= 80, down[0], down[2])
        ).astype(bf16)
        edge_low[at, 128:256] = down[3].astype(bf16)

    def row_copy(source, target, index, other):
        return pltpu.make_async_remote_copy(
            src_ref=source, dst_ref=target, send_sem=h_send.at[index],
            recv_sem=h_recv.at[index], device_id=(other, slab), device_id_type=MESH,
        )

    rows_left = lambda: row_copy(edge_high, halo_high, 0, part - 1)
    rows_right = lambda: row_copy(edge_low, halo_low, 1, part + 1)
    pl.when(left)(lambda: rows_left().start())
    pl.when(right)(lambda: rows_right().start())

    def out_copy(y, land, peer, source, sems):
        return pltpu.make_async_remote_copy(
            src_ref=y.at[rows_of(peer), :], dst_ref=land.at[source],
            send_sem=sems[0].at[peer], recv_sem=sems[1].at[source],
            device_id=(peer, slab), device_id_type=MESH,
        )

    def start_out(y, land, sems):
        for step in (2, 3, 4, 5, 6, 7, 1):
            out_copy(y, land, group_of(step), part, sems).start()

    def leave_out(y, land, sems):
        for step in range(1, groups):
            out_copy(y, land, group_of(step), part, sems).wait_send()

    def arrive_out(y, land, sems):
        for step in range(1, groups):
            out_copy(y, land, part, group_of(step), sems).wait_recv()

    o1_sems, o2_sems = (o1_send, o1_recv), (o2_send, o2_recv)
    start_out(y1, land1, o1_sems)
    own1 = pltpu.make_async_copy(y1.at[rows_of(part), :], land1.at[part], self_sem)
    own1.start()

    pl.when(left)(lambda: rows_right().wait_recv())
    pl.when(right)(lambda: rows_left().wait_recv())

    @pl.loop(0, 16)
    def _(block):
        at = pl.ds(pl.multiple_of(block * 16, 16), 16)
        tile = [y1[at, t * 128 : t * 128 + 128].astype(f32) for t in (2, 4, 6)]
        high, high_b = (halo_high[at, t : t + 128].astype(f32) for t in (0, 128))
        low, low_b = (halo_low[at, t : t + 128].astype(f32) for t in (0, 128))
        x2[1, at, 0:256] = y1[at, 0:256]
        x2[1, at, 256:384] = jnp.where(
            tile_lane < 32, tile[0], jnp.where(tile_lane < 80, high, low)
        ).astype(bf16)
        x2[2, at, 0:128] = jnp.where(tile_lane < 32, low_b, tile[0]).astype(bf16)
        x2[2, at, 128:256] = y1[at, 384:512]
        x2[2, at, 256:384] = jnp.where(
            tile_lane < 64, tile[1], jnp.where(tile_lane < 112, high_b, low_b)
        ).astype(bf16)
        x2[3, at, 0:128] = jnp.where(
            tile_lane < 16, high, jnp.where(tile_lane < 64, low, tile[1])
        ).astype(bf16)
        x2[3, at, 128:256] = y1[at, 640:768]
        x2[3, at, 256:384] = jnp.where(tile_lane < 96, tile[2], high).astype(bf16)

    for step in range(groups):
        group = group_of(step)
        arrive_planes(*y_planes(group))
        scale_group(x2, group)
    combine(y2)
    start_out(y2, land2, o2_sems)
    own1.wait()
    own2 = pltpu.make_async_copy(y2.at[rows_of(part), :], land2.at[part], self_sem)
    own2.start()

    def assemble(land, out_ref):
        for plane in range(3):
            carry = None
            for source in range(groups):
                tile, offset = divmod(CELLS * source, 128)
                start = 256 * plane
                block = land[source, 0:own_rows, start : start + WIN].astype(f32)
                if offset != 32 * plane:
                    block = pltpu.roll(block, (offset - 32 * plane) % WIN, 1)
                head = block[:, 0:128]
                if offset:
                    head = jnp.where(tile_lane < offset, carry, head)
                out_ref[plane, :, tile * 128 : tile * 128 + 128] = head.astype(bf16)
                out_ref[plane, :, tile * 128 + 128 : tile * 128 + 256] = block[:, 128:256].astype(bf16)
                carry = block[:, 256:384]
                if offset + CELLS == WIN:
                    out_ref[plane, :, tile * 128 + 256 : tile * 128 + 384] = carry.astype(bf16)

    arrive_out(y1, land1, o1_sems)
    assemble(land1, first_ref)

    leave_planes(*coef_copies)
    for step in range(groups):
        leave_planes(*x_planes(group_of(step)))
        leave_planes(*y_planes(group_of(step)))
    for step in range(1, groups):
        a2a(group_of(step), part).wait_send()
    pl.when(left)(lambda: rows_left().wait_send())
    pl.when(right)(lambda: rows_right().wait_send())
    leave_out(y1, land1, o1_sems)

    own2.wait()
    arrive_out(y2, land2, o2_sems)
    assemble(land2, second_ref)
    leave_out(y2, land2, o2_sems)


def shards(groups, slabs, panels, mean_field, fluctuations, products, triples, owner_slot):
    fields, nnz = 1 + fluctuations.shape[0], products.shape[0]
    entries = -(-nnz // 128) * 128
    panel_planes = jnp.transpose(panels, (1, 0, 2))
    vmem = pl.BlockSpec(memory_space=pltpu.VMEM)
    out = jax.ShapeDtypeStruct(panel_planes.shape, jnp.bfloat16)
    bf16, f32 = jnp.bfloat16, jnp.float32
    dma = pltpu.SemaphoreType.DMA
    first, second = pl.pallas_call(
        functools.partial(kernel, groups, slabs, fields, nnz),
        out_shape=(out, out),
        in_specs=[vmem] * 6,
        out_specs=(vmem, vmem),
        scratch_shapes=[
            pltpu.VMEM((groups, 3, PAD, WIN), bf16),
            pltpu.VMEM((5, ROWS, WIN), bf16),
            pltpu.VMEM((5, ROWS, WIN), bf16),
            pltpu.VMEM((ROWS, FLAT), bf16),
            pltpu.VMEM((ROWS, FLAT), bf16),
            pltpu.VMEM((ROWS, 256), bf16),
            pltpu.VMEM((ROWS, 256), bf16),
            pltpu.VMEM((ROWS, 256), bf16),
            pltpu.VMEM((ROWS, 256), bf16),
            pltpu.VMEM((groups, PAD, FLAT), bf16),
            pltpu.VMEM((groups, PAD, FLAT), bf16),
            pltpu.VMEM((3, 8, WIN), f32),
            pltpu.VMEM((8, WIN), f32),
            pltpu.VMEM((8, WIN), f32),
            pltpu.VMEM((fields, 6, 16, FLAT), CALC),
            pltpu.VMEM((6, 16, FLAT), CALC),
            pltpu.VMEM((3 * ROWS, entries), bf16),
            pltpu.VMEM((ROWS, entries), bf16),
            pltpu.VMEM((ROWS, fields * ROWS), bf16),
            pltpu.VMEM((fields * ROWS, FLAT), bf16),
            dma((groups,)), dma((groups,)), dma,
            dma((2 * groups,)), dma((2 * groups,)), dma((2,)), dma((2,)), dma((2,)), dma((2,)),
            dma((groups,)), dma((groups,)), dma((groups,)), dma((groups,)),
            dma((2 * groups,)), dma((2 * groups,)),
        ],
        compiler_params=pltpu.CompilerParams(
            collective_id=0, has_side_effects=True, vmem_limit_bytes=48 * 1024 * 1024
        ),
    )(panel_planes, mean_field, fluctuations, triples.T, products[None, :], owner_slot[:, None])
    return jnp.transpose(first, (1, 0, 2)), jnp.transpose(second, (1, 0, 2))


def solution(mesh):
    in_specs = (P("chaos", "space", None), P("space", None), P(None, "space", None), P(), P(), P())
    out_specs = (P("chaos", "space", None), P("chaos", "space", None))
    body = functools.partial(shards, mesh.shape["chaos"], mesh.shape["space"])
    return jax.shard_map(body, mesh=mesh, in_specs=in_specs, out_specs=out_specs, check_vma=False)
```

```python
import functools

import jax
import jax.numpy as jnp
from jax import lax
from jax.experimental import pallas as pl
from jax.experimental.pallas import tpu as pltpu
from jax.sharding import PartitionSpec as P

MESH = pl.DeviceIdType.MESH
SIDE = 48
CELLS = 288
WIN = 384
FLAT = 896
PAD = 32
ROWS = 256
HALF = 0.5 * 0.15

AT = (0, 2, 1)
SEND = (1, 2, 3, 4, 6, 5, 7)

ORDER = ((0, 0), (0, 1), (2, 0), (2, 1), (1, 0), (1, 1), (3, 0), (3, 1))


def tile_window(part):
    start = CELLS * part - SIDE
    return start // 128, start % 128


def linear_window(ref, index, part, lane):
    tile, offset = tile_window(part)
    first, last = max(tile, 0), min(tile + 4, 18)
    block = ref[index + (slice(first * 128, last * 128),)].astype(jnp.float32)
    if tile < 0:
        return jnp.where(lane >= SIDE, pltpu.roll(block, SIDE, 1), 0.0)
    if last - first == 3:
        return jnp.where(lane < WIN - SIDE, pltpu.roll(block, WIN - offset, 1), 0.0)
    return pltpu.roll(block, 512 - offset, 1)[:, :WIN]


def flatten(planes, tile_lane):
    a, b, c = planes
    return jnp.concatenate(
        [
            a[:, 0:256],
            jnp.where(tile_lane < 32, a[:, 256:384], b[:, 0:128]),
            b[:, 128:256],
            jnp.where(tile_lane < 64, b[:, 256:384], c[:, 0:128]),
            c[:, 128:384],
        ],
        axis=1,
    )


def kernel(
    groups, slabs, fields, nnz,
    panel_hbm, mean_hbm, fluct_hbm, triple_hbm, product_hbm, slot_hbm,
    first_ref, second_ref,
    panel_ref, mean_ref, fluct_ref, triple_ref, product_ref, slot_ref, load_sem,
    send_buf, x1, x2, y1, y2, edge_low, edge_high, halo_low, halo_high, land1, land2,
    coef, coef_low, coef_high, weight, keep, lines, drops, onehot_rows, onehot_cols, table, scaled,
    a2a_send, a2a_recv, mid_send, mid_recv, self_sem, mid_sem, z_send, z_recv, c_send, c_recv,
    h_send, h_recv, o1_send, o1_recv, o2_send, o2_recv, z2_send, z2_recv,
):
    part = lax.axis_index("chaos")
    slab = lax.axis_index("space")
    own_rows = panel_ref.shape[1]
    has_low, has_high = slab > 0, slab < slabs - 1
    left, right = part > 0, part < groups - 1
    bf16, f32 = jnp.bfloat16, jnp.float32
    chip, core = part // 2, lax.rem(part, 2)

    def group_of(step):
        far, other = ORDER[step]
        return lax.rem(chip + far, groups // 2) * 2 + lax.rem(core + other, 2)

    loads = [
        pltpu.make_async_copy(source, target, load_sem.at[index])
        for index, (source, target) in enumerate(
            (
                (panel_hbm, panel_ref), (mean_hbm, mean_ref), (fluct_hbm, fluct_ref),
                (triple_hbm, triple_ref), (product_hbm, product_ref), (slot_hbm, slot_ref),
            )
        )
    ]
    for load in loads:
        load.start()

    barrier = pltpu.get_barrier_semaphore()
    for step in range(1, groups):
        pl.semaphore_signal(barrier, inc=1, device_id=(group_of(step), slab), device_id_type=MESH)

    @pl.when(has_low)
    def _():
        pl.semaphore_signal(barrier, inc=1, device_id=(part, slab - 1), device_id_type=MESH)

    @pl.when(has_high)
    def _():
        pl.semaphore_signal(barrier, inc=1, device_id=(part, slab + 1), device_id_type=MESH)

    lane = lax.broadcasted_iota(jnp.int32, (1, WIN), 1)
    tile_lane = lax.broadcasted_iota(jnp.int32, (1, 128), 1)
    send_buf[:, :, 16:32, :] = jnp.zeros((groups, 3, 16, WIN), bf16)
    for plane in range(3):
        cell = lax.rem(lax.broadcasted_iota(jnp.int32, (16, WIN), 1) + (WIN - 32 * plane), SIDE)
        keep[plane, 0] = jnp.where(cell < SIDE - 1, 1.0, 0.0).astype(bf16)
        keep[plane, 1] = jnp.where(cell > 0, 1.0, 0.0).astype(bf16)
    loads[0].wait()
    for target in range(groups):
        for plane in range(3):
            block = linear_window(panel_ref, (plane, slice(None)), target, lane)
            block = pltpu.roll(block, (32 * plane - SIDE) % WIN, 1)
            send_buf[target, AT[plane], 0:own_rows, :] = block.astype(bf16)

    for load in loads[1:]:
        load.wait()
    coef[...] = jnp.zeros_like(coef)
    for target in range(groups):
        @pl.when(part == target)
        def _():
            for plane in range(3):
                coef[plane, 0:1, :] = linear_window(mean_ref, (slice(plane, plane + 1),), target, lane)
                for field in range(1, fields):
                    coef[plane, field : field + 1, :] = linear_window(
                        fluct_ref, (field - 1, slice(plane, plane + 1)), target, lane
                    )

    pl.semaphore_wait(barrier, groups - 1 + has_low.astype(jnp.int32) + has_high.astype(jnp.int32))

    def rows_of(group):
        return pl.ds(pl.multiple_of(group * PAD, PAD), PAD)

    def a2a(peer, source):
        return pltpu.make_async_remote_copy(
            src_ref=send_buf.at[peer, pl.ds(0, 2)],
            dst_ref=x1.at[pl.ds(1, 2), rows_of(source), :],
            send_sem=a2a_send.at[peer],
            recv_sem=a2a_recv.at[source],
            device_id=(peer, slab),
            device_id_type=MESH,
        )

    def a2a_middle(peer, source):
        return pltpu.make_async_remote_copy(
            src_ref=send_buf.at[peer, 2],
            dst_ref=x1.at[3, rows_of(source), :],
            send_sem=mid_send.at[peer],
            recv_sem=mid_recv.at[source],
            device_id=(peer, slab),
            device_id_type=MESH,
        )

    own = pltpu.make_async_copy(
        send_buf.at[part, pl.ds(0, 2)], x1.at[pl.ds(1, 2), rows_of(part), :], self_sem
    )
    own_middle = pltpu.make_async_copy(send_buf.at[part, 2], x1.at[3, rows_of(part), :], mid_sem)
    own.start()
    own_middle.start()
    for step in SEND:
        a2a(group_of(step), part).start()
    for step in SEND:
        a2a_middle(group_of(step), part).start()

    def to_slab(source, target, sems, index, other):
        return pltpu.make_async_remote_copy(
            src_ref=source, dst_ref=target, send_sem=sems[0].at[index], recv_sem=sems[1].at[index],
            device_id=(part, other), device_id_type=MESH,
        )

    def start_low(low):
        pl.when(has_low)(lambda: low().start())

    def start_high(high):
        pl.when(has_high)(lambda: high().start())

    def start_planes(low, high):
        start_low(low)
        start_high(high)

    def arrive_planes(low, high):
        pl.when(has_low)(lambda: high().wait_recv())
        pl.when(has_high)(lambda: low().wait_recv())

    def leave_planes(low, high):
        pl.when(has_low)(lambda: low().wait_send())
        pl.when(has_high)(lambda: high().wait_send())

    @pl.when(jnp.logical_not(has_low))
    def _():
        coef_low[...] = jnp.zeros_like(coef_low)
        x1[0] = jnp.zeros(x1.shape[1:], x1.dtype)
        x2[0] = jnp.zeros(x2.shape[1:], x2.dtype)

    @pl.when(jnp.logical_not(has_high))
    def _():
        coef_high[...] = jnp.zeros_like(coef_high)
        x1[4] = jnp.zeros(x1.shape[1:], x1.dtype)
        x2[4] = jnp.zeros(x2.shape[1:], x2.dtype)

    @pl.when(jnp.logical_not(left))
    def _():
        halo_low[...] = jnp.zeros_like(halo_low)

    @pl.when(jnp.logical_not(right))
    def _():
        halo_high[...] = jnp.zeros_like(halo_high)

    c_sems, z_sems, z2_sems = (c_send, c_recv), (z_send, z_recv), (z2_send, z2_recv)
    coef_copies = (
        lambda: to_slab(coef.at[0], coef_high, c_sems, 0, slab - 1),
        lambda: to_slab(coef.at[2], coef_low, c_sems, 1, slab + 1),
    )
    start_planes(*coef_copies)

    def x_planes(group):
        rows = rows_of(group)
        return (
            lambda: to_slab(x1.at[1, rows, :], x1.at[4, rows, :], z_sems, group, slab - 1),
            lambda: to_slab(x1.at[2, rows, :], x1.at[0, rows, :], z_sems, groups + group, slab + 1),
        )

    def y_planes(group):
        rows = rows_of(group)
        return (
            lambda: to_slab(y1.at[rows, pl.ds(0, WIN)], x2.at[4, rows, :], z2_sems, group, slab - 1),
            lambda: to_slab(
                y1.at[rows, pl.ds(FLAT - WIN, WIN)], x2.at[0, rows, :], z2_sems, groups + group, slab + 1
            ),
        )

    def pass_on(step):
        group = group_of(step)
        if step:
            a2a(part, group).wait_recv()
        else:
            own.wait()
        start_planes(*x_planes(group))

    pass_on(0)

    slot = slot_ref[...].reshape(1, slot_ref.shape[0])
    slot = slot + (PAD - own_rows) * (slot // own_rows)
    slot = jnp.broadcast_to(slot.astype(f32), (8, slot_ref.shape[0])).astype(bf16)
    name = lax.broadcasted_iota(jnp.int32, (slot_ref.shape[0], nnz), 0)

    def slots(index):
        hit = jnp.where(name == triple_ref[index : index + 1, :], 1.0, 0.0).astype(bf16)
        return jnp.dot(slot, hit, preferred_element_type=f32)[0:1]

    def wide(line):
        return jnp.broadcast_to(line, (16, nnz)).astype(bf16)

    lines[0, :, 0:nnz] = wide(slots(0))
    column = slots(1)
    value = product_ref[...].reshape(1, nnz)
    top = value.astype(bf16).astype(f32)
    lines[1, :, 0:nnz] = wide(top)
    lines[2, :, 0:nnz] = wide(value - top)
    for field in range(fields):
        lines[3 + field, :, 0:nnz] = wide(jnp.where(triple_ref[2:3, :] == field, column, -1.0))
    last_tile = slice(nnz // 128 * 128, nnz // 128 * 128 + 128)
    onehot_rows[:, last_tile] = jnp.zeros((2 * ROWS, 128), bf16)
    onehot_cols[:, last_tile] = jnp.zeros((ROWS, 128), bf16)
    numbers = lax.broadcasted_iota(jnp.int32, (16, nnz), 0).astype(f32).astype(bf16)

    def spread(line, block, values, target, base):
        at = pl.ds(pl.multiple_of(base + block * 16, 16), 16)
        start = (block * 16).astype(f32).astype(bf16)
        target[at, 0:nnz] = jnp.where(line - start == numbers, values, jnp.zeros_like(values))

    @pl.loop(0, 16)
    def _(block):
        spread(lines[0, :, 0:nnz], block, lines[1, :, 0:nnz], onehot_rows, 0)
        spread(lines[0, :, 0:nnz], block, lines[2, :, 0:nnz], onehot_rows, ROWS)

    def tabulate(start, stop):
        @pl.loop(start, stop)
        def _(field):
            @pl.loop(0, 16)
            def _(block):
                ones = jnp.ones((16, nnz), bf16)
                spread(lines[3 + field, :, 0:nnz], block, ones, onehot_cols, 0)

            pieces = lax.dot_general(
                onehot_rows[...], onehot_cols[...], (((1,), (1,)), ((), ())), preferred_element_type=f32
            )
            table[:, pl.ds(pl.multiple_of(field * ROWS, ROWS), ROWS)] = (
                pieces[0:ROWS] + pieces[ROWS:]
            ).astype(bf16)

    tabulate(0, 2)
    pass_on(1)
    tabulate(2, 4)
    pass_on(2)
    pass_on(3)
    tabulate(4, 6)
    pass_on(4)
    pass_on(6)

    arrive_planes(*coef_copies)
    inside = []
    for plane in range(3):
        cell = lax.rem(lane + (WIN - 32 * plane), SIDE)
        inside.append((cell < SIDE - 1, cell > 0))

    def neighbours(here, plane, above, below):
        up, down = inside[plane]
        return (
            jnp.where(up, pltpu.roll(here, WIN - 1, 1), 0.0),
            jnp.where(down, pltpu.roll(here, 1, 1), 0.0),
            pltpu.roll(here, WIN - SIDE, 1),
            pltpu.roll(here, SIDE, 1),
            above,
            below,
        )

    halves = []
    for plane in range(3):
        turn = lambda block: pltpu.roll(block, (32 * plane - SIDE) % WIN, 1)
        here = turn(coef[plane])
        below = turn(coef_low[...] if plane == 0 else coef[plane - 1])
        above = turn(coef_high[...] if plane == 2 else coef[plane + 1])
        halves.append([HALF * (here + side) for side in neighbours(here, plane, above, below)])
    for face in range(6):
        half = flatten([halves[plane][face] for plane in range(3)], tile_lane)
        for field in range(fields):
            weight[field, face] = jnp.broadcast_to(half[field : field + 1], (8, FLAT)).astype(bf16)

    pass_on(5)
    pass_on(7)
    tabulate(6, 7)

    def scale_group(x, group):
        for block in range(PAD // 16):
            at = pl.ds(pl.multiple_of(group * PAD + block * 16, 16), 16)
            to = slice(block * 16, block * 16 + 16)
            own_planes = [x[1 + AT[plane], at, :] for plane in range(3)]
            for plane in range(3):
                here = own_planes[plane]
                if plane == 2:
                    above = pltpu.roll(x[4, at, :], 64, 1)
                else:
                    above = pltpu.roll(own_planes[plane + 1], WIN - 32, 1)
                if plane == 0:
                    below = pltpu.roll(x[0, at, :], WIN - 64, 1)
                else:
                    below = pltpu.roll(own_planes[plane - 1], 32, 1)
                sides = (
                    pltpu.roll(here, WIN - 1, 1) * keep[plane, 0],
                    pltpu.roll(here, 1, 1) * keep[plane, 1],
                    pltpu.roll(here, WIN - SIDE, 1),
                    pltpu.roll(here, SIDE, 1),
                    above,
                    below,
                )
                for face, side in enumerate(sides):
                    drop = here - side
                    first, cut = CELLS * plane - 32 * plane, 32 * plane
                    for low in (0, 128, 256):
                        begin, end = max(low, cut), min(low + 128, cut + CELLS)
                        if plane == 2 and low == 256:
                            end = WIN
                        drops[face, to, first + begin : first + end] = drop[:, begin:end]

        @pl.when(group >= 0)
        def _():
            for first in range(0, FLAT, 256):
                lanes = slice(first, min(first + 256, FLAT))
                drop = [drops[face, :, lanes].reshape(PAD // 8, 8, -1) for face in range(6)]
                for field in range(fields):
                    terms = [weight[field, face, :, lanes] * drop[face] for face in range(6)]
                    flux = (terms[0] + terms[1]) + (terms[2] + terms[3]) + (terms[4] + terms[5])
                    to = pl.ds(pl.multiple_of(field * ROWS + group * PAD, PAD), PAD)
                    scaled[to, lanes] = flux.reshape(PAD, -1)

    def combine(y, first):
        for start in (first, first + 256):
            lanes = slice(start, min(start + 256, FLAT))
            y[:, lanes] = jnp.dot(table[...], scaled[:, lanes], preferred_element_type=f32).astype(bf16)

    for step in (0, 1, 2, 3, 4, 6, 5, 7):
        group = group_of(step)
        arrive_planes(*x_planes(group))
        if step:
            a2a_middle(part, group).wait_recv()
        else:
            own_middle.wait()
        scale_group(x1, group)
    combine(y1, 0)
    for step in range(groups):
        start_low(y_planes(group_of(step))[0])
    combine(y1, 512)

    for step in range(groups):
        start_high(y_planes(group_of(step))[1])

    @pl.loop(0, 16)
    def _(block):
        at = pl.ds(pl.multiple_of(block * 16, 16), 16)
        tile = [y1[at, t * 128 : t * 128 + 128].astype(f32) for t in range(7)]
        up = [pltpu.roll(tile[t], 32, 1) for t in (0, 4, 2)]
        edge_high[at, 0:128] = jnp.where((tile_lane >= 32) & (tile_lane < 80), up[0], up[1]).astype(bf16)
        edge_high[at, 128:256] = up[2].astype(bf16)
        down = [pltpu.roll(tile[t], 96, 1) for t in (1, 2, 6, 4)]
        edge_low[at, 0:128] = jnp.where(
            tile_lane >= 96, down[1], jnp.where(tile_lane >= 80, down[0], down[2])
        ).astype(bf16)
        edge_low[at, 128:256] = down[3].astype(bf16)

    def row_copy(source, target, index, other):
        return pltpu.make_async_remote_copy(
            src_ref=source, dst_ref=target, send_sem=h_send.at[index],
            recv_sem=h_recv.at[index], device_id=(other, slab), device_id_type=MESH,
        )

    rows_left = lambda: row_copy(edge_high, halo_high, 0, part - 1)
    rows_right = lambda: row_copy(edge_low, halo_low, 1, part + 1)
    pl.when(left)(lambda: rows_left().start())
    pl.when(right)(lambda: rows_right().start())

    def out_copy(y, land, peer, source, sems, lanes=(0, FLAT), shift=0):
        window = pl.ds(lanes[0], lanes[1])
        return pltpu.make_async_remote_copy(
            src_ref=y.at[rows_of(peer), window], dst_ref=land.at[source, :, window],
            send_sem=sems[0].at[shift + peer], recv_sem=sems[1].at[shift + source],
            device_id=(peer, slab), device_id_type=MESH,
        )

    def start_out(y, land, sems, *how):
        for step in (2, 3, 4, 6, 5, 7, 1):
            out_copy(y, land, group_of(step), part, sems, *how).start()

    def leave_out(y, land, sems, *how):
        for step in range(1, groups):
            out_copy(y, land, group_of(step), part, sems, *how).wait_send()

    def arrive_out(y, land, sems, *how):
        for step in range(1, groups):
            out_copy(y, land, part, group_of(step), sems, *how).wait_recv()

    o1_sems, o2_sems = (o1_send, o1_recv), (o2_send, o2_recv)
    pl.when(left)(lambda: rows_right().wait_recv())
    pl.when(right)(lambda: rows_left().wait_recv())

    start_out(y1, land1, o1_sems)
    own1 = pltpu.make_async_copy(y1.at[rows_of(part), :], land1.at[part], self_sem)
    own1.start()

    @pl.loop(0, 16)
    def _(block):
        at = pl.ds(pl.multiple_of(block * 16, 16), 16)
        tile = [y1[at, t * 128 : t * 128 + 128].astype(f32) for t in (2, 4, 6)]
        high, high_b = (halo_high[at, t : t + 128].astype(f32) for t in (0, 128))
        low, low_b = (halo_low[at, t : t + 128].astype(f32) for t in (0, 128))
        x2[1, at, 0:256] = y1[at, 0:256]
        x2[1, at, 256:384] = jnp.where(
            tile_lane < 32, tile[0], jnp.where(tile_lane < 80, high, low)
        ).astype(bf16)
        x2[3, at, 0:128] = jnp.where(tile_lane < 32, low_b, tile[0]).astype(bf16)
        x2[3, at, 128:256] = y1[at, 384:512]
        x2[3, at, 256:384] = jnp.where(
            tile_lane < 64, tile[1], jnp.where(tile_lane < 112, high_b, low_b)
        ).astype(bf16)
        x2[2, at, 0:128] = jnp.where(
            tile_lane < 16, high, jnp.where(tile_lane < 64, low, tile[1])
        ).astype(bf16)
        x2[2, at, 128:256] = y1[at, 640:768]
        x2[2, at, 256:384] = jnp.where(tile_lane < 96, tile[2], high).astype(bf16)

    for step in range(groups):
        group = group_of(step)
        arrive_planes(*y_planes(group))
        scale_group(x2, group)
    begin, end = ((0, 512), 0), ((512, FLAT - 512), groups)
    combine(y2, 0)
    start_out(y2, land2, o2_sems, *begin)
    combine(y2, 512)
    start_out(y2, land2, o2_sems, *end)
    own1.wait()
    own2 = pltpu.make_async_copy(y2.at[rows_of(part), :], land2.at[part], self_sem)
    own2.start()

    def assemble(land, out_ref):
        for plane in range(3):
            carry = None
            for source in range(groups):
                tile, offset = divmod(CELLS * source, 128)
                start = 256 * plane
                block = land[source, 0:own_rows, start : start + WIN].astype(f32)
                if offset != 32 * plane:
                    block = pltpu.roll(block, (offset - 32 * plane) % WIN, 1)
                head = block[:, 0:128]
                if offset:
                    head = jnp.where(tile_lane < offset, carry, head)
                out_ref[plane, :, tile * 128 : tile * 128 + 128] = head.astype(bf16)
                out_ref[plane, :, tile * 128 + 128 : tile * 128 + 256] = block[:, 128:256].astype(bf16)
                carry = block[:, 256:384]
                if offset + CELLS == WIN:
                    out_ref[plane, :, tile * 128 + 256 : tile * 128 + 384] = carry.astype(bf16)

    arrive_out(y1, land1, o1_sems)
    assemble(land1, first_ref)

    leave_planes(*coef_copies)
    for step in range(groups):
        leave_planes(*x_planes(group_of(step)))
        leave_planes(*y_planes(group_of(step)))
    for step in range(1, groups):
        a2a(group_of(step), part).wait_send()
        a2a_middle(group_of(step), part).wait_send()
    pl.when(left)(lambda: rows_left().wait_send())
    pl.when(right)(lambda: rows_right().wait_send())
    leave_out(y1, land1, o1_sems)

    own2.wait()
    for how in (begin, end):
        arrive_out(y2, land2, o2_sems, *how)
    assemble(land2, second_ref)
    for how in (begin, end):
        leave_out(y2, land2, o2_sems, *how)


def shards(groups, slabs, panels, mean_field, fluctuations, products, triples, owner_slot):
    fields, nnz = 1 + fluctuations.shape[0], products.shape[0]
    entries = -(-nnz // 128) * 128
    panel_planes = jnp.transpose(panels, (1, 0, 2))
    vmem = pl.BlockSpec(memory_space=pltpu.VMEM)
    out = jax.ShapeDtypeStruct(panel_planes.shape, jnp.bfloat16)
    bf16, f32 = jnp.bfloat16, jnp.float32
    dma = pltpu.SemaphoreType.DMA
    operands = (panel_planes, mean_field, fluctuations, triples.T, products, owner_slot)
    first, second = pl.pallas_call(
        functools.partial(kernel, groups, slabs, fields, nnz),
        out_shape=(out, out),
        in_specs=[pl.BlockSpec(memory_space=pltpu.HBM)] * 6,
        out_specs=(vmem, vmem),
        scratch_shapes=[
            pltpu.VMEM(panel_planes.shape, bf16),
            pltpu.VMEM(mean_field.shape, f32),
            pltpu.VMEM(fluctuations.shape, f32),
            pltpu.VMEM((3, nnz), jnp.int32),
            pltpu.VMEM((nnz,), f32),
            pltpu.VMEM(owner_slot.shape, jnp.int32),
            dma((6,)),
            pltpu.VMEM((groups, 3, PAD, WIN), bf16),
            pltpu.VMEM((5, ROWS, WIN), bf16),
            pltpu.VMEM((5, ROWS, WIN), bf16),
            pltpu.VMEM((ROWS, FLAT), bf16),
            pltpu.VMEM((ROWS, FLAT), bf16),
            pltpu.VMEM((ROWS, 256), bf16),
            pltpu.VMEM((ROWS, 256), bf16),
            pltpu.VMEM((ROWS, 256), bf16),
            pltpu.VMEM((ROWS, 256), bf16),
            pltpu.VMEM((groups, PAD, FLAT), bf16),
            pltpu.VMEM((groups, PAD, FLAT), bf16),
            pltpu.VMEM((3, 8, WIN), f32),
            pltpu.VMEM((8, WIN), f32),
            pltpu.VMEM((8, WIN), f32),
            pltpu.VMEM((fields, 6, 8, FLAT), bf16),
            pltpu.VMEM((3, 2, 16, WIN), bf16),
            pltpu.VMEM((3 + fields, 16, entries), bf16),
            pltpu.VMEM((6, PAD, FLAT), bf16),
            pltpu.VMEM((2 * ROWS, entries), bf16),
            pltpu.VMEM((ROWS, entries), bf16),
            pltpu.VMEM((ROWS, fields * ROWS), bf16),
            pltpu.VMEM((fields * ROWS, FLAT), bf16),
            dma((groups,)), dma((groups,)), dma((groups,)), dma((groups,)), dma, dma,
            dma((2 * groups,)), dma((2 * groups,)), dma((2,)), dma((2,)), dma((2,)), dma((2,)),
            dma((groups,)), dma((groups,)), dma((2 * groups,)), dma((2 * groups,)),
            dma((2 * groups,)), dma((2 * groups,)),
        ],
        compiler_params=pltpu.CompilerParams(
            collective_id=0, has_side_effects=True, vmem_limit_bytes=48 * 1024 * 1024
        ),
    )(*(pltpu.with_memory_space_constraint(operand, pltpu.HBM) for operand in operands))
    return jnp.transpose(first, (1, 0, 2)), jnp.transpose(second, (1, 0, 2))


def solution(mesh):
    in_specs = (P("chaos", "space", None), P("space", None), P(None, "space", None), P(), P(), P())
    out_specs = (P("chaos", "space", None), P("chaos", "space", None))
    body = functools.partial(shards, mesh.shape["chaos"], mesh.shape["space"])
    return jax.shard_map(body, mesh=mesh, in_specs=in_specs, out_specs=out_specs, check_vma=False)
```

```python
import functools

import jax
import jax.numpy as jnp
from jax import lax
from jax.experimental import pallas as pl
from jax.experimental.pallas import tpu as pltpu
from jax.sharding import PartitionSpec as P

MESH = pl.DeviceIdType.MESH
SIDE = 48
CELLS = 288
WIN = 384
FLAT = 896
PAD = 32
ROWS = 256
HALF = 0.5 * 0.15

AT = (0, 2, 1)
SEND = (1, 2, 3, 4, 6, 5, 7)
OUT1 = 2

ORDER = ((0, 0), (0, 1), (2, 0), (2, 1), (1, 0), (1, 1), (3, 0), (3, 1))


def tile_window(part):
    start = CELLS * part - SIDE
    return start // 128, start % 128


def linear_window(ref, index, part, lane):
    tile, offset = tile_window(part)
    first, last = max(tile, 0), min(tile + 4, 18)
    block = ref[index + (slice(first * 128, last * 128),)].astype(jnp.float32)
    if tile < 0:
        return jnp.where(lane >= SIDE, pltpu.roll(block, SIDE, 1), 0.0)
    if last - first == 3:
        return jnp.where(lane < WIN - SIDE, pltpu.roll(block, WIN - offset, 1), 0.0)
    return pltpu.roll(block, 512 - offset, 1)[:, :WIN]


def flatten(planes, tile_lane):
    a, b, c = planes
    return jnp.concatenate(
        [
            a[:, 0:256],
            jnp.where(tile_lane < 32, a[:, 256:384], b[:, 0:128]),
            b[:, 128:256],
            jnp.where(tile_lane < 64, b[:, 256:384], c[:, 0:128]),
            c[:, 128:384],
        ],
        axis=1,
    )


def kernel(
    groups, slabs, fields, nnz,
    panel_hbm, mean_hbm, fluct_hbm, triple_hbm, product_hbm, slot_hbm,
    first_ref, second_ref,
    panel_ref, mean_ref, fluct_ref, triple_ref, product_ref, slot_ref, load_sem,
    send_buf, x1, x2, y1, y2, edge_low, edge_high, halo_low, halo_high, land1, land2,
    coef, coef_low, coef_high, weight, keep, lines, drops, onehot_rows, onehot_cols, table, scaled,
    a2a_send, a2a_recv, mid_send, mid_recv, self_sem, mid_sem, z_send, z_recv, c_send, c_recv,
    h_send, h_recv, o1_send, o1_recv, o2_send, o2_recv, z2_send, z2_recv,
):
    part = lax.axis_index("chaos")
    slab = lax.axis_index("space")
    own_rows = panel_ref.shape[1]
    has_low, has_high = slab > 0, slab < slabs - 1
    left, right = part > 0, part < groups - 1
    bf16, f32 = jnp.bfloat16, jnp.float32
    chip, core = part // 2, lax.rem(part, 2)

    def group_of(step):
        far, other = ORDER[step]
        return lax.rem(chip + far, groups // 2) * 2 + lax.rem(core + other, 2)

    loads = [
        pltpu.make_async_copy(source, target, load_sem.at[index])
        for index, (source, target) in enumerate(
            (
                (panel_hbm, panel_ref), (mean_hbm, mean_ref), (fluct_hbm, fluct_ref),
                (triple_hbm, triple_ref), (product_hbm, product_ref), (slot_hbm, slot_ref),
            )
        )
    ]
    for load in loads:
        load.start()

    barrier = pltpu.get_barrier_semaphore()
    for step in range(1, groups):
        pl.semaphore_signal(barrier, inc=1, device_id=(group_of(step), slab), device_id_type=MESH)

    @pl.when(has_low)
    def _():
        pl.semaphore_signal(barrier, inc=1, device_id=(part, slab - 1), device_id_type=MESH)

    @pl.when(has_high)
    def _():
        pl.semaphore_signal(barrier, inc=1, device_id=(part, slab + 1), device_id_type=MESH)

    lane = lax.broadcasted_iota(jnp.int32, (1, WIN), 1)
    tile_lane = lax.broadcasted_iota(jnp.int32, (1, 128), 1)
    send_buf[:, :, 16:32, :] = jnp.zeros((groups, 3, 16, WIN), bf16)
    for plane in range(3):
        cell = lax.rem(lax.broadcasted_iota(jnp.int32, (16, WIN), 1) + (WIN - 32 * plane), SIDE)
        keep[plane, 0] = jnp.where(cell < SIDE - 1, 1.0, 0.0).astype(bf16)
        keep[plane, 1] = jnp.where(cell > 0, 1.0, 0.0).astype(bf16)
    loads[0].wait()
    for target in range(groups):
        for plane in range(3):
            block = linear_window(panel_ref, (plane, slice(None)), target, lane)
            block = pltpu.roll(block, (32 * plane - SIDE) % WIN, 1)
            send_buf[target, AT[plane], 0:own_rows, :] = block.astype(bf16)

    pl.semaphore_wait(barrier, groups - 1 + has_low.astype(jnp.int32) + has_high.astype(jnp.int32))

    def rows_of(group):
        return pl.ds(pl.multiple_of(group * PAD, PAD), PAD)

    def a2a(peer, source):
        return pltpu.make_async_remote_copy(
            src_ref=send_buf.at[peer, pl.ds(0, 2)],
            dst_ref=x1.at[pl.ds(1, 2), rows_of(source), :],
            send_sem=a2a_send.at[peer],
            recv_sem=a2a_recv.at[source],
            device_id=(peer, slab),
            device_id_type=MESH,
        )

    def a2a_middle(peer, source):
        return pltpu.make_async_remote_copy(
            src_ref=send_buf.at[peer, 2],
            dst_ref=x1.at[3, rows_of(source), :],
            send_sem=mid_send.at[peer],
            recv_sem=mid_recv.at[source],
            device_id=(peer, slab),
            device_id_type=MESH,
        )

    own = pltpu.make_async_copy(
        send_buf.at[part, pl.ds(0, 2)], x1.at[pl.ds(1, 2), rows_of(part), :], self_sem
    )
    own_middle = pltpu.make_async_copy(send_buf.at[part, 2], x1.at[3, rows_of(part), :], mid_sem)
    own.start()
    own_middle.start()
    for step in SEND:
        a2a(group_of(step), part).start()
    for step in SEND:
        a2a_middle(group_of(step), part).start()

    for load in loads[1:]:
        load.wait()
    coef[...] = jnp.zeros_like(coef)
    for target in range(groups):
        @pl.when(part == target)
        def _():
            for plane in range(3):
                coef[plane, 0:1, :] = linear_window(mean_ref, (slice(plane, plane + 1),), target, lane)
                for field in range(1, fields):
                    coef[plane, field : field + 1, :] = linear_window(
                        fluct_ref, (field - 1, slice(plane, plane + 1)), target, lane
                    )

    def to_slab(source, target, sems, index, other):
        return pltpu.make_async_remote_copy(
            src_ref=source, dst_ref=target, send_sem=sems[0].at[index], recv_sem=sems[1].at[index],
            device_id=(part, other), device_id_type=MESH,
        )

    def start_low(low):
        pl.when(has_low)(lambda: low().start())

    def start_high(high):
        pl.when(has_high)(lambda: high().start())

    def start_planes(low, high):
        start_low(low)
        start_high(high)

    def arrive_planes(low, high):
        pl.when(has_low)(lambda: high().wait_recv())
        pl.when(has_high)(lambda: low().wait_recv())

    def leave_planes(low, high):
        pl.when(has_low)(lambda: low().wait_send())
        pl.when(has_high)(lambda: high().wait_send())

    @pl.when(jnp.logical_not(has_low))
    def _():
        coef_low[...] = jnp.zeros_like(coef_low)
        x1[0] = jnp.zeros(x1.shape[1:], x1.dtype)
        x2[0] = jnp.zeros(x2.shape[1:], x2.dtype)

    @pl.when(jnp.logical_not(has_high))
    def _():
        coef_high[...] = jnp.zeros_like(coef_high)
        x1[4] = jnp.zeros(x1.shape[1:], x1.dtype)
        x2[4] = jnp.zeros(x2.shape[1:], x2.dtype)

    @pl.when(jnp.logical_not(left))
    def _():
        halo_low[...] = jnp.zeros_like(halo_low)

    @pl.when(jnp.logical_not(right))
    def _():
        halo_high[...] = jnp.zeros_like(halo_high)

    c_sems, z_sems, z2_sems = (c_send, c_recv), (z_send, z_recv), (z2_send, z2_recv)
    coef_copies = (
        lambda: to_slab(coef.at[0], coef_high, c_sems, 0, slab - 1),
        lambda: to_slab(coef.at[2], coef_low, c_sems, 1, slab + 1),
    )
    start_planes(*coef_copies)

    def x_planes(group):
        rows = rows_of(group)
        return (
            lambda: to_slab(x1.at[1, rows, :], x1.at[4, rows, :], z_sems, group, slab - 1),
            lambda: to_slab(x1.at[2, rows, :], x1.at[0, rows, :], z_sems, groups + group, slab + 1),
        )

    def y_planes(group):
        rows = rows_of(group)
        return (
            lambda: to_slab(y1.at[rows, pl.ds(0, WIN)], x2.at[4, rows, :], z2_sems, group, slab - 1),
            lambda: to_slab(
                y1.at[rows, pl.ds(FLAT - WIN, WIN)], x2.at[0, rows, :], z2_sems, groups + group, slab + 1
            ),
        )

    def pass_on(step):
        group = group_of(step)
        if step:
            a2a(part, group).wait_recv()
        else:
            own.wait()
        start_planes(*x_planes(group))

    pass_on(0)

    slot = slot_ref[...].reshape(1, slot_ref.shape[0])
    slot = slot + (PAD - own_rows) * (slot // own_rows)
    slot = jnp.broadcast_to(slot.astype(f32), (8, slot_ref.shape[0])).astype(bf16)
    name = lax.broadcasted_iota(jnp.int32, (slot_ref.shape[0], nnz), 0)

    def slots(index):
        hit = jnp.where(name == triple_ref[index : index + 1, :], 1.0, 0.0).astype(bf16)
        return jnp.dot(slot, hit, preferred_element_type=f32)[0:1]

    def wide(line):
        return jnp.broadcast_to(line, (16, nnz)).astype(bf16)

    lines[0, :, 0:nnz] = wide(slots(0))
    column = slots(1)
    value = product_ref[...].reshape(1, nnz)
    top = value.astype(bf16).astype(f32)
    lines[1, :, 0:nnz] = wide(top)
    lines[2, :, 0:nnz] = wide(value - top)
    for field in range(fields):
        lines[3 + field, :, 0:nnz] = wide(jnp.where(triple_ref[2:3, :] == field, column, -1.0))
    last_tile = slice(nnz // 128 * 128, nnz // 128 * 128 + 128)
    onehot_rows[:, last_tile] = jnp.zeros((2 * ROWS, 128), bf16)
    onehot_cols[:, last_tile] = jnp.zeros((ROWS, 128), bf16)
    numbers = lax.broadcasted_iota(jnp.int32, (16, nnz), 0).astype(f32).astype(bf16)

    def spread(line, block, values, target, base):
        at = pl.ds(pl.multiple_of(base + block * 16, 16), 16)
        start = (block * 16).astype(f32).astype(bf16)
        target[at, 0:nnz] = jnp.where(line - start == numbers, values, jnp.zeros_like(values))

    @pl.loop(0, 8)
    def _(pair):
        for block in (2 * pair, 2 * pair + 1):
            spread(lines[0, :, 0:nnz], block, lines[1, :, 0:nnz], onehot_rows, 0)
            spread(lines[0, :, 0:nnz], block, lines[2, :, 0:nnz], onehot_rows, ROWS)

    def tabulate(start, stop):
        @pl.loop(start, stop)
        def _(field):
            @pl.loop(0, 4)
            def _(four):
                ones = jnp.ones((16, nnz), bf16)
                for block in range(4):
                    spread(lines[3 + field, :, 0:nnz], 4 * four + block, ones, onehot_cols, 0)

            pieces = lax.dot_general(
                onehot_rows[...], onehot_cols[...], (((1,), (1,)), ((), ())), preferred_element_type=f32
            )
            table[:, pl.ds(pl.multiple_of(field * ROWS, ROWS), ROWS)] = (
                pieces[0:ROWS] + pieces[ROWS:]
            ).astype(bf16)

    tabulate(0, 2)
    pass_on(1)
    tabulate(2, 4)
    pass_on(2)
    pass_on(3)
    tabulate(4, 6)
    pass_on(4)
    pass_on(6)

    arrive_planes(*coef_copies)
    inside = []
    for plane in range(3):
        cell = lax.rem(lane + (WIN - 32 * plane), SIDE)
        inside.append((cell < SIDE - 1, cell > 0))

    def neighbours(here, plane, above, below):
        up, down = inside[plane]
        return (
            jnp.where(up, pltpu.roll(here, WIN - 1, 1), 0.0),
            jnp.where(down, pltpu.roll(here, 1, 1), 0.0),
            pltpu.roll(here, WIN - SIDE, 1),
            pltpu.roll(here, SIDE, 1),
            above,
            below,
        )

    halves = []
    for plane in range(3):
        turn = lambda block: pltpu.roll(block, (32 * plane - SIDE) % WIN, 1)
        here = turn(coef[plane])
        below = turn(coef_low[...] if plane == 0 else coef[plane - 1])
        above = turn(coef_high[...] if plane == 2 else coef[plane + 1])
        halves.append([HALF * (here + side) for side in neighbours(here, plane, above, below)])
    for face in range(6):
        half = flatten([halves[plane][face] for plane in range(3)], tile_lane)
        for field in range(fields):
            weight[field, face] = jnp.broadcast_to(half[field : field + 1], (8, FLAT)).astype(bf16)

    pass_on(5)
    pass_on(7)
    tabulate(6, 7)

    def scale_group(x, group):
        for block in range(PAD // 16):
            at = pl.ds(pl.multiple_of(group * PAD + block * 16, 16), 16)
            to = slice(block * 16, block * 16 + 16)
            own_planes = [x[1 + AT[plane], at, :] for plane in range(3)]
            for plane in range(3):
                here = own_planes[plane]
                if plane == 2:
                    above = pltpu.roll(x[4, at, :], 64, 1)
                else:
                    above = pltpu.roll(own_planes[plane + 1], WIN - 32, 1)
                if plane == 0:
                    below = pltpu.roll(x[0, at, :], WIN - 64, 1)
                else:
                    below = pltpu.roll(own_planes[plane - 1], 32, 1)
                sides = (
                    pltpu.roll(here, WIN - 1, 1) * keep[plane, 0],
                    pltpu.roll(here, 1, 1) * keep[plane, 1],
                    pltpu.roll(here, WIN - SIDE, 1),
                    pltpu.roll(here, SIDE, 1),
                    above,
                    below,
                )
                for face, side in enumerate(sides):
                    drop = here - side
                    first, cut = CELLS * plane - 32 * plane, 32 * plane
                    for low in (0, 128, 256):
                        begin, end = max(low, cut), min(low + 128, cut + CELLS)
                        if plane == 2 and low == 256:
                            end = WIN
                        drops[face, to, first + begin : first + end] = drop[:, begin:end]

        @pl.when(part >= 0)
        def _():
            for first in range(0, FLAT, 256):
                lanes = slice(first, min(first + 256, FLAT))
                drop = [drops[face, :, lanes].reshape(PAD // 8, 8, -1) for face in range(6)]
                for field in range(fields):
                    terms = [weight[field, face, :, lanes] * drop[face] for face in range(6)]
                    flux = (terms[0] + terms[1]) + (terms[2] + terms[3]) + (terms[4] + terms[5])
                    to = pl.ds(pl.multiple_of(field * ROWS + group * PAD, PAD), PAD)
                    scaled[to, lanes] = flux.reshape(PAD, -1)

    def combine(y, first):
        for start in (first, first + 256):
            lanes = slice(start, min(start + 256, FLAT))
            y[:, lanes] = jnp.dot(table[...], scaled[:, lanes], preferred_element_type=f32).astype(bf16)

    for step in (0, 1, 2, 3, 4, 6, 5, 7):
        group = group_of(step)
        arrive_planes(*x_planes(group))
        if step:
            a2a_middle(part, group).wait_recv()
        else:
            own_middle.wait()
        scale_group(x1, group)
    combine(y1, 0)
    for group in range(groups):
        start_low(y_planes(group)[0])
    combine(y1, 512)

    for step in range(groups):
        start_high(y_planes(step)[1])

    def row_copy(source, target, index, other, group):
        rows = rows_of(group)
        return pltpu.make_async_remote_copy(
            src_ref=source.at[rows, :], dst_ref=target.at[rows, :],
            send_sem=h_send.at[index * groups + group], recv_sem=h_recv.at[index * groups + group],
            device_id=(other, slab), device_id_type=MESH,
        )

    def rows_left(group):
        return row_copy(edge_high, halo_high, 0, part - 1, group)

    def rows_right(group):
        return row_copy(edge_low, halo_low, 1, part + 1, group)

    for group in range(groups):
        at = pl.ds(group * PAD, PAD)
        tile = [y1[at, t * 128 : t * 128 + 128].astype(f32) for t in range(7)]
        up = [pltpu.roll(tile[t], 32, 1) for t in (0, 4, 2)]
        edge_high[at, 0:128] = jnp.where((tile_lane >= 32) & (tile_lane < 80), up[0], up[1]).astype(bf16)
        edge_high[at, 128:256] = up[2].astype(bf16)
        down = [pltpu.roll(tile[t], 96, 1) for t in (1, 2, 6, 4)]
        edge_low[at, 0:128] = jnp.where(
            tile_lane >= 96, down[1], jnp.where(tile_lane >= 80, down[0], down[2])
        ).astype(bf16)
        edge_low[at, 128:256] = down[3].astype(bf16)
        pl.when(left)(lambda: rows_left(group).start())
        pl.when(right)(lambda: rows_right(group).start())

    def out_copy(y, land, peer, source, sems, lanes=(0, FLAT), shift=0):
        window = pl.ds(lanes[0], lanes[1])
        return pltpu.make_async_remote_copy(
            src_ref=y.at[rows_of(peer), window], dst_ref=land.at[source, :, window],
            send_sem=sems[0].at[shift + peer], recv_sem=sems[1].at[shift + source],
            device_id=(peer, slab), device_id_type=MESH,
        )

    def start_out(y, land, sems, *how):
        for step in (2, 3, 4, 6, 5, 7, 1):
            out_copy(y, land, group_of(step), part, sems, *how).start()

    def leave_out(y, land, sems, *how):
        for step in range(1, groups):
            out_copy(y, land, group_of(step), part, sems, *how).wait_send()

    def arrive_out(y, land, sems, *how):
        for step in range(1, groups):
            out_copy(y, land, part, group_of(step), sems, *how).wait_recv()

    o1_sems, o2_sems = (o1_send, o1_recv), (o2_send, o2_recv)
    def windows(group):
        at = pl.ds(group * PAD, PAD)
        tile = [y1[at, t * 128 : t * 128 + 128].astype(f32) for t in (2, 4, 6)]
        high, high_b = (halo_high[at, t : t + 128].astype(f32) for t in (0, 128))
        low, low_b = (halo_low[at, t : t + 128].astype(f32) for t in (0, 128))
        x2[1, at, 0:256] = y1[at, 0:256]
        x2[1, at, 256:384] = jnp.where(
            tile_lane < 32, tile[0], jnp.where(tile_lane < 80, high, low)
        ).astype(bf16)
        x2[3, at, 0:128] = jnp.where(tile_lane < 32, low_b, tile[0]).astype(bf16)
        x2[3, at, 128:256] = y1[at, 384:512]
        x2[3, at, 256:384] = jnp.where(
            tile_lane < 64, tile[1], jnp.where(tile_lane < 112, high_b, low_b)
        ).astype(bf16)
        x2[2, at, 0:128] = jnp.where(
            tile_lane < 16, high, jnp.where(tile_lane < 64, low, tile[1])
        ).astype(bf16)
        x2[2, at, 128:256] = y1[at, 640:768]
        x2[2, at, 256:384] = jnp.where(tile_lane < 96, tile[2], high).astype(bf16)

    own1 = pltpu.make_async_copy(y1.at[rows_of(part), :], land1.at[part], self_sem)
    for group in range(groups):
        pl.when(left)(lambda: rows_right(group).wait_recv())
        pl.when(right)(lambda: rows_left(group).wait_recv())
        windows(group)
        if group == OUT1:
            start_out(y1, land1, o1_sems)
            own1.start()
        arrive_planes(*y_planes(group))
        scale_group(x2, group)
    begin, end = ((0, 512), 0), ((512, FLAT - 512), groups)
    combine(y2, 0)
    start_out(y2, land2, o2_sems, *begin)
    combine(y2, 512)
    start_out(y2, land2, o2_sems, *end)
    own1.wait()
    own2 = pltpu.make_async_copy(y2.at[rows_of(part), :], land2.at[part], self_sem)
    own2.start()

    def assemble(land, out_ref, planes):
        for plane in planes:
            carry = None
            for source in range(groups):
                tile, offset = divmod(CELLS * source, 128)
                start = 256 * plane
                block = land[source, 0:own_rows, start : start + WIN].astype(f32)
                if offset != 32 * plane:
                    block = pltpu.roll(block, (offset - 32 * plane) % WIN, 1)
                head = block[:, 0:128]
                if offset:
                    head = jnp.where(tile_lane < offset, carry, head)
                out_ref[plane, :, tile * 128 : tile * 128 + 128] = head.astype(bf16)
                out_ref[plane, :, tile * 128 + 128 : tile * 128 + 256] = block[:, 128:256].astype(bf16)
                carry = block[:, 256:384]
                if offset + CELLS == WIN:
                    out_ref[plane, :, tile * 128 + 256 : tile * 128 + 384] = carry.astype(bf16)

    arrive_out(y1, land1, o1_sems)
    assemble(land1, first_ref, range(3))

    leave_planes(*coef_copies)
    for step in range(groups):
        leave_planes(*x_planes(group_of(step)))
        leave_planes(*y_planes(step))
        pl.when(left)(lambda: rows_left(step).wait_send())
        pl.when(right)(lambda: rows_right(step).wait_send())
    for step in range(1, groups):
        a2a(group_of(step), part).wait_send()
        a2a_middle(group_of(step), part).wait_send()
    leave_out(y1, land1, o1_sems)

    own2.wait()
    arrive_out(y2, land2, o2_sems, *begin)
    assemble(land2, second_ref, (0,))
    arrive_out(y2, land2, o2_sems, *end)
    assemble(land2, second_ref, (1, 2))
    for how in (begin, end):
        leave_out(y2, land2, o2_sems, *how)


def shards(groups, slabs, panels, mean_field, fluctuations, products, triples, owner_slot):
    fields, nnz = 1 + fluctuations.shape[0], products.shape[0]
    entries = -(-nnz // 128) * 128
    panel_planes = jnp.transpose(panels, (1, 0, 2))
    vmem = pl.BlockSpec(memory_space=pltpu.VMEM)
    out = jax.ShapeDtypeStruct(panel_planes.shape, jnp.bfloat16)
    bf16, f32 = jnp.bfloat16, jnp.float32
    dma = pltpu.SemaphoreType.DMA
    operands = (panel_planes, mean_field, fluctuations, triples.T, products, owner_slot)
    first, second = pl.pallas_call(
        functools.partial(kernel, groups, slabs, fields, nnz),
        out_shape=(out, out),
        in_specs=[pl.BlockSpec(memory_space=pltpu.HBM)] * 6,
        out_specs=(vmem, vmem),
        scratch_shapes=[
            pltpu.VMEM(panel_planes.shape, bf16),
            pltpu.VMEM(mean_field.shape, f32),
            pltpu.VMEM(fluctuations.shape, f32),
            pltpu.VMEM((3, nnz), jnp.int32),
            pltpu.VMEM((nnz,), f32),
            pltpu.VMEM(owner_slot.shape, jnp.int32),
            dma((6,)),
            pltpu.VMEM((groups, 3, PAD, WIN), bf16),
            pltpu.VMEM((5, ROWS, WIN), bf16),
            pltpu.VMEM((5, ROWS, WIN), bf16),
            pltpu.VMEM((ROWS, FLAT), bf16),
            pltpu.VMEM((ROWS, FLAT), bf16),
            pltpu.VMEM((ROWS, 256), bf16),
            pltpu.VMEM((ROWS, 256), bf16),
            pltpu.VMEM((ROWS, 256), bf16),
            pltpu.VMEM((ROWS, 256), bf16),
            pltpu.VMEM((groups, PAD, FLAT), bf16),
            pltpu.VMEM((groups, PAD, FLAT), bf16),
            pltpu.VMEM((3, 8, WIN), f32),
            pltpu.VMEM((8, WIN), f32),
            pltpu.VMEM((8, WIN), f32),
            pltpu.VMEM((fields, 6, 8, FLAT), bf16),
            pltpu.VMEM((3, 2, 16, WIN), bf16),
            pltpu.VMEM((3 + fields, 16, entries), bf16),
            pltpu.VMEM((6, PAD, FLAT), bf16),
            pltpu.VMEM((2 * ROWS, entries), bf16),
            pltpu.VMEM((ROWS, entries), bf16),
            pltpu.VMEM((ROWS, fields * ROWS), bf16),
            pltpu.VMEM((fields * ROWS, FLAT), bf16),
            dma((groups,)), dma((groups,)), dma((groups,)), dma((groups,)), dma, dma,
            dma((2 * groups,)), dma((2 * groups,)), dma((2,)), dma((2,)), dma((2 * groups,)), dma((2 * groups,)),
            dma((groups,)), dma((groups,)), dma((2 * groups,)), dma((2 * groups,)),
            dma((2 * groups,)), dma((2 * groups,)),
        ],
        compiler_params=pltpu.CompilerParams(
            collective_id=0, has_side_effects=True, vmem_limit_bytes=48 * 1024 * 1024
        ),
    )(*(pltpu.with_memory_space_constraint(operand, pltpu.HBM) for operand in operands))
    return jnp.transpose(first, (1, 0, 2)), jnp.transpose(second, (1, 0, 2))


def solution(mesh):
    in_specs = (P("chaos", "space", None), P("space", None), P(None, "space", None), P(), P(), P())
    out_specs = (P("chaos", "space", None), P("chaos", "space", None))
    body = functools.partial(shards, mesh.shape["chaos"], mesh.shape["space"])
    return jax.shard_map(body, mesh=mesh, in_specs=in_specs, out_specs=out_specs, check_vma=False)
```

```python
import functools

import jax
import jax.numpy as jnp
from jax import lax
from jax.experimental import pallas as pl
from jax.experimental.pallas import tpu as pltpu
from jax.sharding import PartitionSpec as P

MESH = pl.DeviceIdType.MESH
SIDE = 48
CELLS = 288
WIN = 384
FLAT = 896
PAD = 32
ROWS = 256
HALF = 0.5 * 0.15

AT = (0, 2, 1)
SEND = (1, 2, 3, 4, 6, 5, 7)
OUT1 = 1

ORDER = ((0, 0), (0, 1), (2, 0), (2, 1), (1, 0), (1, 1), (3, 0), (3, 1))


def tile_window(part):
    start = CELLS * part - SIDE
    return start // 128, start % 128


def linear_window(ref, index, part, lane):
    tile, offset = tile_window(part)
    first, last = max(tile, 0), min(tile + 4, 18)
    block = ref[index + (slice(first * 128, last * 128),)].astype(jnp.float32)
    if tile < 0:
        return jnp.where(lane >= SIDE, pltpu.roll(block, SIDE, 1), 0.0)
    if last - first == 3:
        return jnp.where(lane < WIN - SIDE, pltpu.roll(block, WIN - offset, 1), 0.0)
    return pltpu.roll(block, 512 - offset, 1)[:, :WIN]


def flatten(planes, tile_lane):
    a, b, c = planes
    return jnp.concatenate(
        [
            a[:, 0:256],
            jnp.where(tile_lane < 32, a[:, 256:384], b[:, 0:128]),
            b[:, 128:256],
            jnp.where(tile_lane < 64, b[:, 256:384], c[:, 0:128]),
            c[:, 128:384],
        ],
        axis=1,
    )


def kernel(
    groups, slabs, fields, nnz,
    panel_hbm, mean_hbm, fluct_hbm, triple_hbm, product_hbm, slot_hbm,
    first_ref, second_ref,
    panel_ref, mean_ref, fluct_ref, triple_ref, product_ref, slot_ref, load_sem,
    send_buf, x1, x2, y1, y2, edge_low, edge_high, halo_low, halo_high, land1, land2,
    coef, coef_low, coef_high, weight, keep, lines, drops, onehot_rows, onehot_cols, table, scaled,
    a2a_send, a2a_recv, mid_send, mid_recv, self_sem, mid_sem, z_send, z_recv, c_send, c_recv,
    h_send, h_recv, o1_send, o1_recv, o2_send, o2_recv, z2_send, z2_recv,
):
    part = lax.axis_index("chaos")
    slab = lax.axis_index("space")
    own_rows = panel_ref.shape[1]
    has_low, has_high = slab > 0, slab < slabs - 1
    left, right = part > 0, part < groups - 1
    bf16, f32 = jnp.bfloat16, jnp.float32
    chip, core = part // 2, lax.rem(part, 2)

    def group_of(step):
        far, other = ORDER[step]
        return lax.rem(chip + far, groups // 2) * 2 + lax.rem(core + other, 2)

    loads = [
        pltpu.make_async_copy(source, target, load_sem.at[index])
        for index, (source, target) in enumerate(
            (
                (panel_hbm, panel_ref), (mean_hbm, mean_ref), (fluct_hbm, fluct_ref),
                (triple_hbm, triple_ref), (product_hbm, product_ref), (slot_hbm, slot_ref),
            )
        )
    ]
    for load in loads:
        load.start()

    barrier = pltpu.get_barrier_semaphore()
    for step in range(1, groups):
        pl.semaphore_signal(barrier, inc=1, device_id=(group_of(step), slab), device_id_type=MESH)

    @pl.when(has_low)
    def _():
        pl.semaphore_signal(barrier, inc=1, device_id=(part, slab - 1), device_id_type=MESH)

    @pl.when(has_high)
    def _():
        pl.semaphore_signal(barrier, inc=1, device_id=(part, slab + 1), device_id_type=MESH)

    lane = lax.broadcasted_iota(jnp.int32, (1, WIN), 1)
    tile_lane = lax.broadcasted_iota(jnp.int32, (1, 128), 1)
    send_buf[:, :, 16:32, :] = jnp.zeros((groups, 3, 16, WIN), bf16)
    for plane in range(3):
        cell = lax.rem(lax.broadcasted_iota(jnp.int32, (16, WIN), 1) + (WIN - 32 * plane), SIDE)
        keep[plane, 0] = jnp.where(cell < SIDE - 1, 1.0, 0.0).astype(bf16)
        keep[plane, 1] = jnp.where(cell > 0, 1.0, 0.0).astype(bf16)
    loads[0].wait()
    for target in range(groups):
        for plane in range(3):
            block = linear_window(panel_ref, (plane, slice(None)), target, lane)
            block = pltpu.roll(block, (32 * plane - SIDE) % WIN, 1)
            send_buf[target, AT[plane], 0:own_rows, :] = block.astype(bf16)

    pl.semaphore_wait(barrier, groups - 1 + has_low.astype(jnp.int32) + has_high.astype(jnp.int32))

    def rows_of(group):
        return pl.ds(pl.multiple_of(group * PAD, PAD), PAD)

    def a2a(peer, source):
        return pltpu.make_async_remote_copy(
            src_ref=send_buf.at[peer, pl.ds(0, 2)],
            dst_ref=x1.at[pl.ds(1, 2), rows_of(source), :],
            send_sem=a2a_send.at[peer],
            recv_sem=a2a_recv.at[source],
            device_id=(peer, slab),
            device_id_type=MESH,
        )

    def a2a_middle(peer, source):
        return pltpu.make_async_remote_copy(
            src_ref=send_buf.at[peer, 2],
            dst_ref=x1.at[3, rows_of(source), :],
            send_sem=mid_send.at[peer],
            recv_sem=mid_recv.at[source],
            device_id=(peer, slab),
            device_id_type=MESH,
        )

    own = pltpu.make_async_copy(
        send_buf.at[part, pl.ds(0, 2)], x1.at[pl.ds(1, 2), rows_of(part), :], self_sem
    )
    own_middle = pltpu.make_async_copy(send_buf.at[part, 2], x1.at[3, rows_of(part), :], mid_sem)
    own.start()
    own_middle.start()
    for step in SEND:
        a2a(group_of(step), part).start()
    for step in SEND:
        a2a_middle(group_of(step), part).start()

    for load in loads[1:]:
        load.wait()
    coef[...] = jnp.zeros_like(coef)
    for target in range(groups):
        @pl.when(part == target)
        def _():
            for plane in range(3):
                coef[plane, 0:1, :] = linear_window(mean_ref, (slice(plane, plane + 1),), target, lane)
                for field in range(1, fields):
                    coef[plane, field : field + 1, :] = linear_window(
                        fluct_ref, (field - 1, slice(plane, plane + 1)), target, lane
                    )

    def to_slab(source, target, sems, index, other):
        return pltpu.make_async_remote_copy(
            src_ref=source, dst_ref=target, send_sem=sems[0].at[index], recv_sem=sems[1].at[index],
            device_id=(part, other), device_id_type=MESH,
        )

    def start_low(low):
        pl.when(has_low)(lambda: low().start())

    def start_high(high):
        pl.when(has_high)(lambda: high().start())

    def start_planes(low, high):
        start_low(low)
        start_high(high)

    def arrive_planes(low, high):
        pl.when(has_low)(lambda: high().wait_recv())
        pl.when(has_high)(lambda: low().wait_recv())

    def leave_planes(low, high):
        pl.when(has_low)(lambda: low().wait_send())
        pl.when(has_high)(lambda: high().wait_send())

    @pl.when(jnp.logical_not(has_low))
    def _():
        coef_low[...] = jnp.zeros_like(coef_low)
        x1[0] = jnp.zeros(x1.shape[1:], x1.dtype)
        x2[0] = jnp.zeros(x2.shape[1:], x2.dtype)

    @pl.when(jnp.logical_not(has_high))
    def _():
        coef_high[...] = jnp.zeros_like(coef_high)
        x1[4] = jnp.zeros(x1.shape[1:], x1.dtype)
        x2[4] = jnp.zeros(x2.shape[1:], x2.dtype)

    @pl.when(jnp.logical_not(left))
    def _():
        halo_low[...] = jnp.zeros_like(halo_low)

    @pl.when(jnp.logical_not(right))
    def _():
        halo_high[...] = jnp.zeros_like(halo_high)

    c_sems, z_sems, z2_sems = (c_send, c_recv), (z_send, z_recv), (z2_send, z2_recv)
    coef_copies = (
        lambda: to_slab(coef.at[0], coef_high, c_sems, 0, slab - 1),
        lambda: to_slab(coef.at[2], coef_low, c_sems, 1, slab + 1),
    )
    start_planes(*coef_copies)

    def x_planes(group):
        rows = rows_of(group)
        return (
            lambda: to_slab(x1.at[1, rows, :], x1.at[4, rows, :], z_sems, group, slab - 1),
            lambda: to_slab(x1.at[2, rows, :], x1.at[0, rows, :], z_sems, groups + group, slab + 1),
        )

    def y_planes(group):
        rows = rows_of(group)
        return (
            lambda: to_slab(y1.at[rows, pl.ds(0, WIN)], x2.at[4, rows, :], z2_sems, group, slab - 1),
            lambda: to_slab(
                y1.at[rows, pl.ds(FLAT - WIN, WIN)], x2.at[0, rows, :], z2_sems, groups + group, slab + 1
            ),
        )

    def pass_on(step):
        group = group_of(step)
        if step:
            a2a(part, group).wait_recv()
        else:
            own.wait()
        start_planes(*x_planes(group))

    pass_on(0)

    slot = slot_ref[...].reshape(1, slot_ref.shape[0])
    slot = slot + (PAD - own_rows) * (slot // own_rows)
    slot = jnp.broadcast_to(slot.astype(f32), (8, slot_ref.shape[0])).astype(bf16)
    name = lax.broadcasted_iota(jnp.int32, (slot_ref.shape[0], nnz), 0)

    def slots(index):
        hit = jnp.where(name == triple_ref[index : index + 1, :], 1.0, 0.0).astype(bf16)
        return jnp.dot(slot, hit, preferred_element_type=f32)[0:1]

    def wide(line):
        return jnp.broadcast_to(line, (16, nnz)).astype(bf16)

    lines[0, :, 0:nnz] = wide(slots(0))
    column = slots(1)
    value = product_ref[...].reshape(1, nnz)
    top = value.astype(bf16).astype(f32)
    lines[1, :, 0:nnz] = wide(top)
    lines[2, :, 0:nnz] = wide(value - top)
    for field in range(fields):
        lines[3 + field, :, 0:nnz] = wide(jnp.where(triple_ref[2:3, :] == field, column, -1.0))
    last_tile = slice(nnz // 128 * 128, nnz // 128 * 128 + 128)
    onehot_rows[:, last_tile] = jnp.zeros((2 * ROWS, 128), bf16)
    onehot_cols[:, last_tile] = jnp.zeros((ROWS, 128), bf16)
    numbers = lax.broadcasted_iota(jnp.int32, (16, nnz), 0).astype(f32).astype(bf16)

    def spread(line, block, values, target, base):
        at = pl.ds(pl.multiple_of(base + block * 16, 16), 16)
        start = (block * 16).astype(f32).astype(bf16)
        target[at, 0:nnz] = jnp.where(line - start == numbers, values, jnp.zeros_like(values))

    @pl.loop(0, 8)
    def _(pair):
        for block in (2 * pair, 2 * pair + 1):
            spread(lines[0, :, 0:nnz], block, lines[1, :, 0:nnz], onehot_rows, 0)
            spread(lines[0, :, 0:nnz], block, lines[2, :, 0:nnz], onehot_rows, ROWS)

    def tabulate(start, stop):
        @pl.loop(start, stop)
        def _(field):
            @pl.loop(0, 4)
            def _(four):
                ones = jnp.ones((16, nnz), bf16)
                for block in range(4):
                    spread(lines[3 + field, :, 0:nnz], 4 * four + block, ones, onehot_cols, 0)

            pieces = lax.dot_general(
                onehot_rows[...], onehot_cols[...], (((1,), (1,)), ((), ())), preferred_element_type=f32
            )
            table[:, pl.ds(pl.multiple_of(field * ROWS, ROWS), ROWS)] = (
                pieces[0:ROWS] + pieces[ROWS:]
            ).astype(bf16)

    tabulate(0, 3)
    pass_on(1)
    tabulate(3, 5)
    for step in (2, 3, 4, 6):
        pass_on(step)
    tabulate(5, 6)

    arrive_planes(*coef_copies)
    inside = []
    for plane in range(3):
        cell = lax.rem(lane + (WIN - 32 * plane), SIDE)
        inside.append((cell < SIDE - 1, cell > 0))

    def neighbours(here, plane, above, below):
        up, down = inside[plane]
        return (
            jnp.where(up, pltpu.roll(here, WIN - 1, 1), 0.0),
            jnp.where(down, pltpu.roll(here, 1, 1), 0.0),
            pltpu.roll(here, WIN - SIDE, 1),
            pltpu.roll(here, SIDE, 1),
            above,
            below,
        )

    halves = []
    for plane in range(3):
        turn = lambda block: pltpu.roll(block, (32 * plane - SIDE) % WIN, 1)
        here = turn(coef[plane])
        below = turn(coef_low[...] if plane == 0 else coef[plane - 1])
        above = turn(coef_high[...] if plane == 2 else coef[plane + 1])
        halves.append([HALF * (here + side) for side in neighbours(here, plane, above, below)])
    for face in range(6):
        half = flatten([halves[plane][face] for plane in range(3)], tile_lane)
        for field in range(fields):
            weight[field, face] = jnp.broadcast_to(half[field : field + 1], (8, FLAT)).astype(bf16)

    pass_on(5)
    pass_on(7)
    tabulate(6, 7)

    def scale_group(x, group):
        for block in range(PAD // 16):
            at = pl.ds(pl.multiple_of(group * PAD + block * 16, 16), 16)
            to = slice(block * 16, block * 16 + 16)
            own_planes = [x[1 + AT[plane], at, :] for plane in range(3)]
            for plane in range(3):
                here = own_planes[plane]
                if plane == 2:
                    above = pltpu.roll(x[4, at, :], 64, 1)
                else:
                    above = pltpu.roll(own_planes[plane + 1], WIN - 32, 1)
                if plane == 0:
                    below = pltpu.roll(x[0, at, :], WIN - 64, 1)
                else:
                    below = pltpu.roll(own_planes[plane - 1], 32, 1)
                sides = (
                    pltpu.roll(here, WIN - 1, 1) * keep[plane, 0],
                    pltpu.roll(here, 1, 1) * keep[plane, 1],
                    pltpu.roll(here, WIN - SIDE, 1),
                    pltpu.roll(here, SIDE, 1),
                    above,
                    below,
                )
                for face, side in enumerate(sides):
                    drop = here - side
                    first, cut = CELLS * plane - 32 * plane, 32 * plane
                    for low in (0, 128, 256):
                        begin, end = max(low, cut), min(low + 128, cut + CELLS)
                        if plane == 2 and low == 256:
                            end = WIN
                        drops[face, to, first + begin : first + end] = drop[:, begin:end]

        @pl.when(part >= 0)
        def _():
            for first in range(0, FLAT, 256):
                lanes = slice(first, min(first + 256, FLAT))
                drop = [drops[face, :, lanes].reshape(PAD // 8, 8, -1) for face in range(6)]
                for field in range(fields):
                    terms = [weight[field, face, :, lanes] * drop[face] for face in range(6)]
                    flux = (terms[0] + terms[1]) + (terms[2] + terms[3]) + (terms[4] + terms[5])
                    to = pl.ds(pl.multiple_of(field * ROWS + group * PAD, PAD), PAD)
                    scaled[to, lanes] = flux.reshape(PAD, -1)

    def combine(y, first):
        for start in (first, first + 256):
            lanes = slice(start, min(start + 256, FLAT))
            y[:, lanes] = jnp.dot(table[...], scaled[:, lanes], preferred_element_type=f32).astype(bf16)

    for step in (0, 1, 2, 3, 4, 6, 5, 7):
        group = group_of(step)
        arrive_planes(*x_planes(group))
        if step:
            a2a_middle(part, group).wait_recv()
        else:
            own_middle.wait()
        scale_group(x1, group)
    combine(y1, 0)
    for group in range(groups):
        start_low(y_planes(group)[0])
    combine(y1, 512)

    for step in range(groups):
        start_high(y_planes(step)[1])

    def row_copy(source, target, index, other, group):
        rows = rows_of(group)
        return pltpu.make_async_remote_copy(
            src_ref=source.at[rows, :], dst_ref=target.at[rows, :],
            send_sem=h_send.at[index * groups + group], recv_sem=h_recv.at[index * groups + group],
            device_id=(other, slab), device_id_type=MESH,
        )

    def rows_left(group):
        return row_copy(edge_high, halo_high, 0, part - 1, group)

    def rows_right(group):
        return row_copy(edge_low, halo_low, 1, part + 1, group)

    for group in range(groups):
        at = pl.ds(group * PAD, PAD)
        tile = [y1[at, t * 128 : t * 128 + 128].astype(f32) for t in range(7)]
        up = [pltpu.roll(tile[t], 32, 1) for t in (0, 4, 2)]
        edge_high[at, 0:128] = jnp.where((tile_lane >= 32) & (tile_lane < 80), up[0], up[1]).astype(bf16)
        edge_high[at, 128:256] = up[2].astype(bf16)
        down = [pltpu.roll(tile[t], 96, 1) for t in (1, 2, 6, 4)]
        edge_low[at, 0:128] = jnp.where(
            tile_lane >= 96, down[1], jnp.where(tile_lane >= 80, down[0], down[2])
        ).astype(bf16)
        edge_low[at, 128:256] = down[3].astype(bf16)
        pl.when(left)(lambda: rows_left(group).start())
        pl.when(right)(lambda: rows_right(group).start())

    def out_copy(y, land, peer, source, sems, lanes=(0, FLAT), shift=0):
        window = pl.ds(lanes[0], lanes[1])
        return pltpu.make_async_remote_copy(
            src_ref=y.at[rows_of(peer), window], dst_ref=land.at[source, :, window],
            send_sem=sems[0].at[shift + peer], recv_sem=sems[1].at[shift + source],
            device_id=(peer, slab), device_id_type=MESH,
        )

    def start_out(y, land, sems, *how):
        for step in (2, 3, 4, 6, 5, 7, 1):
            out_copy(y, land, group_of(step), part, sems, *how).start()

    def leave_out(y, land, sems, *how):
        for step in range(1, groups):
            out_copy(y, land, group_of(step), part, sems, *how).wait_send()

    def arrive_out(y, land, sems, *how):
        for step in range(1, groups):
            out_copy(y, land, part, group_of(step), sems, *how).wait_recv()

    o1_sems, o2_sems = (o1_send, o1_recv), (o2_send, o2_recv)
    def windows(group):
        at = pl.ds(group * PAD, PAD)
        tile = [y1[at, t * 128 : t * 128 + 128].astype(f32) for t in (2, 4, 6)]
        high, high_b = (halo_high[at, t : t + 128].astype(f32) for t in (0, 128))
        low, low_b = (halo_low[at, t : t + 128].astype(f32) for t in (0, 128))
        x2[1, at, 0:256] = y1[at, 0:256]
        x2[1, at, 256:384] = jnp.where(
            tile_lane < 32, tile[0], jnp.where(tile_lane < 80, high, low)
        ).astype(bf16)
        x2[3, at, 0:128] = jnp.where(tile_lane < 32, low_b, tile[0]).astype(bf16)
        x2[3, at, 128:256] = y1[at, 384:512]
        x2[3, at, 256:384] = jnp.where(
            tile_lane < 64, tile[1], jnp.where(tile_lane < 112, high_b, low_b)
        ).astype(bf16)
        x2[2, at, 0:128] = jnp.where(
            tile_lane < 16, high, jnp.where(tile_lane < 64, low, tile[1])
        ).astype(bf16)
        x2[2, at, 128:256] = y1[at, 640:768]
        x2[2, at, 256:384] = jnp.where(tile_lane < 96, tile[2], high).astype(bf16)

    own1 = pltpu.make_async_copy(y1.at[rows_of(part), :], land1.at[part], self_sem)
    for group in range(groups):
        pl.when(left)(lambda: rows_right(group).wait_recv())
        pl.when(right)(lambda: rows_left(group).wait_recv())
        windows(group)
        if group == OUT1:
            start_out(y1, land1, o1_sems)
            own1.start()
        arrive_planes(*y_planes(group))
        scale_group(x2, group)
    begin, end = ((0, 512), 0), ((512, FLAT - 512), groups)
    combine(y2, 0)
    start_out(y2, land2, o2_sems, *begin)
    combine(y2, 512)
    start_out(y2, land2, o2_sems, *end)
    own1.wait()
    own2 = pltpu.make_async_copy(y2.at[rows_of(part), :], land2.at[part], self_sem)
    own2.start()

    def assemble(land, out_ref, planes):
        for plane in planes:
            carry = None
            for source in range(groups):
                tile, offset = divmod(CELLS * source, 128)
                start = 256 * plane
                block = land[source, 0:own_rows, start : start + WIN].astype(f32)
                if offset != 32 * plane:
                    block = pltpu.roll(block, (offset - 32 * plane) % WIN, 1)
                head = block[:, 0:128]
                if offset:
                    head = jnp.where(tile_lane < offset, carry, head)
                out_ref[plane, :, tile * 128 : tile * 128 + 128] = head.astype(bf16)
                out_ref[plane, :, tile * 128 + 128 : tile * 128 + 256] = block[:, 128:256].astype(bf16)
                carry = block[:, 256:384]
                if offset + CELLS == WIN:
                    out_ref[plane, :, tile * 128 + 256 : tile * 128 + 384] = carry.astype(bf16)

    arrive_out(y1, land1, o1_sems)
    assemble(land1, first_ref, range(3))

    leave_planes(*coef_copies)
    for step in range(groups):
        leave_planes(*x_planes(group_of(step)))
        leave_planes(*y_planes(step))
        pl.when(left)(lambda: rows_left(step).wait_send())
        pl.when(right)(lambda: rows_right(step).wait_send())
    for step in range(1, groups):
        a2a(group_of(step), part).wait_send()
        a2a_middle(group_of(step), part).wait_send()
    leave_out(y1, land1, o1_sems)

    own2.wait()
    arrive_out(y2, land2, o2_sems, *begin)
    assemble(land2, second_ref, (0,))
    arrive_out(y2, land2, o2_sems, *end)
    assemble(land2, second_ref, (1, 2))
    for how in (begin, end):
        leave_out(y2, land2, o2_sems, *how)


def shards(groups, slabs, panels, mean_field, fluctuations, products, triples, owner_slot):
    fields, nnz = 1 + fluctuations.shape[0], products.shape[0]
    entries = -(-nnz // 128) * 128
    panel_planes = jnp.transpose(panels, (1, 0, 2))
    vmem = pl.BlockSpec(memory_space=pltpu.VMEM)
    out = jax.ShapeDtypeStruct(panel_planes.shape, jnp.bfloat16)
    bf16, f32 = jnp.bfloat16, jnp.float32
    dma = pltpu.SemaphoreType.DMA
    operands = (panel_planes, mean_field, fluctuations, triples.T, products, owner_slot)
    first, second = pl.pallas_call(
        functools.partial(kernel, groups, slabs, fields, nnz),
        out_shape=(out, out),
        in_specs=[pl.BlockSpec(memory_space=pltpu.HBM)] * 6,
        out_specs=(vmem, vmem),
        scratch_shapes=[
            pltpu.VMEM(panel_planes.shape, bf16),
            pltpu.VMEM(mean_field.shape, f32),
            pltpu.VMEM(fluctuations.shape, f32),
            pltpu.VMEM((3, nnz), jnp.int32),
            pltpu.VMEM((nnz,), f32),
            pltpu.VMEM(owner_slot.shape, jnp.int32),
            dma((6,)),
            pltpu.VMEM((groups, 3, PAD, WIN), bf16),
            pltpu.VMEM((5, ROWS, WIN), bf16),
            pltpu.VMEM((5, ROWS, WIN), bf16),
            pltpu.VMEM((ROWS, FLAT), bf16),
            pltpu.VMEM((ROWS, FLAT), bf16),
            pltpu.VMEM((ROWS, 256), bf16),
            pltpu.VMEM((ROWS, 256), bf16),
            pltpu.VMEM((ROWS, 256), bf16),
            pltpu.VMEM((ROWS, 256), bf16),
            pltpu.VMEM((groups, PAD, FLAT), bf16),
            pltpu.VMEM((groups, PAD, FLAT), bf16),
            pltpu.VMEM((3, 8, WIN), f32),
            pltpu.VMEM((8, WIN), f32),
            pltpu.VMEM((8, WIN), f32),
            pltpu.VMEM((fields, 6, 8, FLAT), bf16),
            pltpu.VMEM((3, 2, 16, WIN), bf16),
            pltpu.VMEM((3 + fields, 16, entries), bf16),
            pltpu.VMEM((6, PAD, FLAT), bf16),
            pltpu.VMEM((2 * ROWS, entries), bf16),
            pltpu.VMEM((ROWS, entries), bf16),
            pltpu.VMEM((ROWS, fields * ROWS), bf16),
            pltpu.VMEM((fields * ROWS, FLAT), bf16),
            dma((groups,)), dma((groups,)), dma((groups,)), dma((groups,)), dma, dma,
            dma((2 * groups,)), dma((2 * groups,)), dma((2,)), dma((2,)), dma((2 * groups,)), dma((2 * groups,)),
            dma((groups,)), dma((groups,)), dma((2 * groups,)), dma((2 * groups,)),
            dma((2 * groups,)), dma((2 * groups,)),
        ],
        compiler_params=pltpu.CompilerParams(
            collective_id=0, has_side_effects=True, vmem_limit_bytes=48 * 1024 * 1024
        ),
    )(*(pltpu.with_memory_space_constraint(operand, pltpu.HBM) for operand in operands))
    return jnp.transpose(first, (1, 0, 2)), jnp.transpose(second, (1, 0, 2))


def solution(mesh):
    in_specs = (P("chaos", "space", None), P("space", None), P(None, "space", None), P(), P(), P())
    out_specs = (P("chaos", "space", None), P("chaos", "space", None))
    body = functools.partial(shards, mesh.shape["chaos"], mesh.shape["space"])
    return jax.shard_map(body, mesh=mesh, in_specs=in_specs, out_specs=out_specs, check_vma=False)
```

```python
import functools

import jax
import jax.numpy as jnp
from jax import lax
from jax.experimental import pallas as pl
from jax.experimental.pallas import tpu as pltpu
from jax.sharding import PartitionSpec as P

MESH = pl.DeviceIdType.MESH
SIDE = 48
CELLS = 288
WIN = 384
FLAT = 896
PAD = 32
ROWS = 256
HALF = 0.5 * 0.15

AT = (0, 2, 1)
SEND = (1, 2, 3, 4, 6, 5, 7)
OUT1 = 0

ORDER = ((0, 0), (0, 1), (2, 0), (2, 1), (1, 0), (1, 1), (3, 0), (3, 1))


def tile_window(part):
    start = CELLS * part - SIDE
    return start // 128, start % 128


def linear_window(ref, index, part, lane):
    tile, offset = tile_window(part)
    first, last = max(tile, 0), min(tile + 4, 18)
    block = ref[index + (slice(first * 128, last * 128),)].astype(jnp.float32)
    if tile < 0:
        return jnp.where(lane >= SIDE, pltpu.roll(block, SIDE, 1), 0.0)
    if last - first == 3:
        return jnp.where(lane < WIN - SIDE, pltpu.roll(block, WIN - offset, 1), 0.0)
    return pltpu.roll(block, 512 - offset, 1)[:, :WIN]


def flatten(planes, tile_lane):
    a, b, c = planes
    return jnp.concatenate(
        [
            a[:, 0:256],
            jnp.where(tile_lane < 32, a[:, 256:384], b[:, 0:128]),
            b[:, 128:256],
            jnp.where(tile_lane < 64, b[:, 256:384], c[:, 0:128]),
            c[:, 128:384],
        ],
        axis=1,
    )


def kernel(
    groups, slabs, fields, nnz,
    panel_hbm, mean_hbm, fluct_hbm, triple_hbm, product_hbm, slot_hbm,
    first_ref, second_ref,
    panel_ref, mean_ref, fluct_ref, triple_ref, product_ref, slot_ref, load_sem,
    send_buf, x1, x2, y1, y2, edge_low, edge_high, halo_low, halo_high, land1, land2,
    coef, coef_low, coef_high, weight, keep, lines, drops, onehot_rows, onehot_cols, table, scaled,
    a2a_send, a2a_recv, mid_send, mid_recv, self_sem, mid_sem, z_send, z_recv, c_send, c_recv,
    h_send, h_recv, o1_send, o1_recv, o2_send, o2_recv, z2_send, z2_recv,
):
    part = lax.axis_index("chaos")
    slab = lax.axis_index("space")
    own_rows = panel_ref.shape[1]
    has_low, has_high = slab > 0, slab < slabs - 1
    left, right = part > 0, part < groups - 1
    bf16, f32 = jnp.bfloat16, jnp.float32
    chip, core = part // 2, lax.rem(part, 2)

    def group_of(step):
        far, other = ORDER[step]
        return lax.rem(chip + far, groups // 2) * 2 + lax.rem(core + other, 2)

    loads = [
        pltpu.make_async_copy(source, target, load_sem.at[index])
        for index, (source, target) in enumerate(
            (
                (panel_hbm, panel_ref), (mean_hbm, mean_ref), (fluct_hbm, fluct_ref),
                (triple_hbm, triple_ref), (product_hbm, product_ref), (slot_hbm, slot_ref),
            )
        )
    ]
    for load in loads:
        load.start()

    barrier = pltpu.get_barrier_semaphore()
    for step in range(1, groups):
        pl.semaphore_signal(barrier, inc=1, device_id=(group_of(step), slab), device_id_type=MESH)

    @pl.when(has_low)
    def _():
        pl.semaphore_signal(barrier, inc=1, device_id=(part, slab - 1), device_id_type=MESH)

    @pl.when(has_high)
    def _():
        pl.semaphore_signal(barrier, inc=1, device_id=(part, slab + 1), device_id_type=MESH)

    lane = lax.broadcasted_iota(jnp.int32, (1, WIN), 1)
    tile_lane = lax.broadcasted_iota(jnp.int32, (1, 128), 1)
    send_buf[:, :, 16:32, :] = jnp.zeros((groups, 3, 16, WIN), bf16)
    for plane in range(3):
        cell = lax.rem(lax.broadcasted_iota(jnp.int32, (16, WIN), 1) + (WIN - 32 * plane), SIDE)
        keep[plane, 0] = jnp.where(cell < SIDE - 1, 1.0, 0.0).astype(bf16)
        keep[plane, 1] = jnp.where(cell > 0, 1.0, 0.0).astype(bf16)
    loads[0].wait()
    for target in range(groups):
        for plane in range(3):
            block = linear_window(panel_ref, (plane, slice(None)), target, lane)
            block = pltpu.roll(block, (32 * plane - SIDE) % WIN, 1)
            send_buf[target, AT[plane], 0:own_rows, :] = block.astype(bf16)

    pl.semaphore_wait(barrier, groups - 1 + has_low.astype(jnp.int32) + has_high.astype(jnp.int32))

    def rows_of(group):
        return pl.ds(pl.multiple_of(group * PAD, PAD), PAD)

    def a2a(peer, source):
        return pltpu.make_async_remote_copy(
            src_ref=send_buf.at[peer, pl.ds(0, 2)],
            dst_ref=x1.at[pl.ds(1, 2), rows_of(source), :],
            send_sem=a2a_send.at[peer],
            recv_sem=a2a_recv.at[source],
            device_id=(peer, slab),
            device_id_type=MESH,
        )

    def a2a_middle(peer, source):
        return pltpu.make_async_remote_copy(
            src_ref=send_buf.at[peer, 2],
            dst_ref=x1.at[3, rows_of(source), :],
            send_sem=mid_send.at[peer],
            recv_sem=mid_recv.at[source],
            device_id=(peer, slab),
            device_id_type=MESH,
        )

    own = pltpu.make_async_copy(
        send_buf.at[part, pl.ds(0, 2)], x1.at[pl.ds(1, 2), rows_of(part), :], self_sem
    )
    own_middle = pltpu.make_async_copy(send_buf.at[part, 2], x1.at[3, rows_of(part), :], mid_sem)
    own.start()
    own_middle.start()
    for step in SEND:
        a2a(group_of(step), part).start()
    for step in SEND:
        a2a_middle(group_of(step), part).start()

    for load in loads[1:]:
        load.wait()
    coef[...] = jnp.zeros_like(coef)
    for target in range(groups):
        @pl.when(part == target)
        def _():
            for plane in range(3):
                coef[plane, 0:1, :] = linear_window(mean_ref, (slice(plane, plane + 1),), target, lane)
                for field in range(1, fields):
                    coef[plane, field : field + 1, :] = linear_window(
                        fluct_ref, (field - 1, slice(plane, plane + 1)), target, lane
                    )

    def to_slab(source, target, sems, index, other):
        return pltpu.make_async_remote_copy(
            src_ref=source, dst_ref=target, send_sem=sems[0].at[index], recv_sem=sems[1].at[index],
            device_id=(part, other), device_id_type=MESH,
        )

    def start_low(low):
        pl.when(has_low)(lambda: low().start())

    def start_high(high):
        pl.when(has_high)(lambda: high().start())

    def start_planes(low, high):
        start_low(low)
        start_high(high)

    def arrive_planes(low, high):
        pl.when(has_low)(lambda: high().wait_recv())
        pl.when(has_high)(lambda: low().wait_recv())

    def leave_planes(low, high):
        pl.when(has_low)(lambda: low().wait_send())
        pl.when(has_high)(lambda: high().wait_send())

    @pl.when(jnp.logical_not(has_low))
    def _():
        coef_low[...] = jnp.zeros_like(coef_low)
        x1[0] = jnp.zeros(x1.shape[1:], x1.dtype)
        x2[0] = jnp.zeros(x2.shape[1:], x2.dtype)

    @pl.when(jnp.logical_not(has_high))
    def _():
        coef_high[...] = jnp.zeros_like(coef_high)
        x1[4] = jnp.zeros(x1.shape[1:], x1.dtype)
        x2[4] = jnp.zeros(x2.shape[1:], x2.dtype)

    @pl.when(jnp.logical_not(left))
    def _():
        halo_low[...] = jnp.zeros_like(halo_low)

    @pl.when(jnp.logical_not(right))
    def _():
        halo_high[...] = jnp.zeros_like(halo_high)

    c_sems, z_sems, z2_sems = (c_send, c_recv), (z_send, z_recv), (z2_send, z2_recv)
    coef_copies = (
        lambda: to_slab(coef.at[0], coef_high, c_sems, 0, slab - 1),
        lambda: to_slab(coef.at[2], coef_low, c_sems, 1, slab + 1),
    )
    start_planes(*coef_copies)

    def x_planes(group):
        rows = rows_of(group)
        return (
            lambda: to_slab(x1.at[1, rows, :], x1.at[4, rows, :], z_sems, group, slab - 1),
            lambda: to_slab(x1.at[2, rows, :], x1.at[0, rows, :], z_sems, groups + group, slab + 1),
        )

    def y_planes(group):
        rows = rows_of(group)
        return (
            lambda: to_slab(y1.at[rows, pl.ds(0, WIN)], x2.at[4, rows, :], z2_sems, group, slab - 1),
            lambda: to_slab(
                y1.at[rows, pl.ds(FLAT - WIN, WIN)], x2.at[0, rows, :], z2_sems, groups + group, slab + 1
            ),
        )

    def pass_on(step):
        group = group_of(step)
        if step:
            a2a(part, group).wait_recv()
        else:
            own.wait()
        start_planes(*x_planes(group))

    pass_on(0)

    slot = slot_ref[...].reshape(1, slot_ref.shape[0])
    slot = slot + (PAD - own_rows) * (slot // own_rows)
    slot = jnp.broadcast_to(slot.astype(f32), (8, slot_ref.shape[0])).astype(bf16)
    name = lax.broadcasted_iota(jnp.int32, (slot_ref.shape[0], nnz), 0)

    def slots(index):
        hit = jnp.where(name == triple_ref[index : index + 1, :], 1.0, 0.0).astype(bf16)
        return jnp.dot(slot, hit, preferred_element_type=f32)[0:1]

    def wide(line):
        return jnp.broadcast_to(line, (16, nnz)).astype(bf16)

    lines[0, :, 0:nnz] = wide(slots(0))
    column = slots(1)
    value = product_ref[...].reshape(1, nnz)
    top = value.astype(bf16).astype(f32)
    lines[1, :, 0:nnz] = wide(top)
    lines[2, :, 0:nnz] = wide(value - top)
    for field in range(fields):
        lines[3 + field, :, 0:nnz] = wide(jnp.where(triple_ref[2:3, :] == field, column, -1.0))
    last_tile = slice(nnz // 128 * 128, nnz // 128 * 128 + 128)
    onehot_rows[:, last_tile] = jnp.zeros((2 * ROWS, 128), bf16)
    onehot_cols[:, last_tile] = jnp.zeros((ROWS, 128), bf16)
    numbers = lax.broadcasted_iota(jnp.int32, (16, nnz), 0).astype(f32).astype(bf16)

    def spread(line, block, values, target, base):
        at = pl.ds(pl.multiple_of(base + block * 16, 16), 16)
        start = (block * 16).astype(f32).astype(bf16)
        target[at, 0:nnz] = jnp.where(line - start == numbers, values, jnp.zeros_like(values))

    @pl.loop(0, 8)
    def _(pair):
        for block in (2 * pair, 2 * pair + 1):
            spread(lines[0, :, 0:nnz], block, lines[1, :, 0:nnz], onehot_rows, 0)
            spread(lines[0, :, 0:nnz], block, lines[2, :, 0:nnz], onehot_rows, ROWS)

    def tabulate(start, stop):
        @pl.loop(start, stop)
        def _(field):
            @pl.loop(0, 4)
            def _(four):
                ones = jnp.ones((16, nnz), bf16)
                for block in range(4):
                    spread(lines[3 + field, :, 0:nnz], 4 * four + block, ones, onehot_cols, 0)

            pieces = lax.dot_general(
                onehot_rows[...], onehot_cols[...], (((1,), (1,)), ((), ())), preferred_element_type=f32
            )
            table[:, pl.ds(pl.multiple_of(field * ROWS, ROWS), ROWS)] = (
                pieces[0:ROWS] + pieces[ROWS:]
            ).astype(bf16)

    tabulate(0, 3)
    pass_on(1)
    tabulate(3, 5)
    for step in (2, 3, 4, 6):
        pass_on(step)
    tabulate(5, 6)

    arrive_planes(*coef_copies)
    inside = []
    for plane in range(3):
        cell = lax.rem(lane + (WIN - 32 * plane), SIDE)
        inside.append((cell < SIDE - 1, cell > 0))

    def neighbours(here, plane, above, below):
        up, down = inside[plane]
        return (
            jnp.where(up, pltpu.roll(here, WIN - 1, 1), 0.0),
            jnp.where(down, pltpu.roll(here, 1, 1), 0.0),
            pltpu.roll(here, WIN - SIDE, 1),
            pltpu.roll(here, SIDE, 1),
            above,
            below,
        )

    halves = []
    for plane in range(3):
        turn = lambda block: pltpu.roll(block, (32 * plane - SIDE) % WIN, 1)
        here = turn(coef[plane])
        below = turn(coef_low[...] if plane == 0 else coef[plane - 1])
        above = turn(coef_high[...] if plane == 2 else coef[plane + 1])
        halves.append([HALF * (here + side) for side in neighbours(here, plane, above, below)])
    for face in range(6):
        half = flatten([halves[plane][face] for plane in range(3)], tile_lane)
        for field in range(fields):
            weight[field, face] = jnp.broadcast_to(half[field : field + 1], (8, FLAT)).astype(bf16)

    pass_on(5)
    pass_on(7)
    tabulate(6, 7)

    def scale_group(x, group):
        for block in range(PAD // 16):
            at = pl.ds(pl.multiple_of(group * PAD + block * 16, 16), 16)
            to = slice(block * 16, block * 16 + 16)
            own_planes = [x[1 + AT[plane], at, :] for plane in range(3)]
            for plane in range(3):
                here = own_planes[plane]
                if plane == 2:
                    above = pltpu.roll(x[4, at, :], 64, 1)
                else:
                    above = pltpu.roll(own_planes[plane + 1], WIN - 32, 1)
                if plane == 0:
                    below = pltpu.roll(x[0, at, :], WIN - 64, 1)
                else:
                    below = pltpu.roll(own_planes[plane - 1], 32, 1)
                sides = (
                    pltpu.roll(here, WIN - 1, 1) * keep[plane, 0],
                    pltpu.roll(here, 1, 1) * keep[plane, 1],
                    pltpu.roll(here, WIN - SIDE, 1),
                    pltpu.roll(here, SIDE, 1),
                    above,
                    below,
                )
                for face, side in enumerate(sides):
                    drop = here - side
                    first, cut = CELLS * plane - 32 * plane, 32 * plane
                    for low in (0, 128, 256):
                        begin, end = max(low, cut), min(low + 128, cut + CELLS)
                        if plane == 2 and low == 256:
                            end = WIN
                        drops[face, to, first + begin : first + end] = drop[:, begin:end]

        @pl.when(part >= 0)
        def _():
            for first in range(0, FLAT, 256):
                lanes = slice(first, min(first + 256, FLAT))
                drop = [drops[face, :, lanes].reshape(PAD // 8, 8, -1) for face in range(6)]
                for field in range(fields):
                    terms = [weight[field, face, :, lanes] * drop[face] for face in range(6)]
                    flux = (terms[0] + terms[1]) + (terms[2] + terms[3]) + (terms[4] + terms[5])
                    to = pl.ds(pl.multiple_of(field * ROWS + group * PAD, PAD), PAD)
                    scaled[to, lanes] = flux.reshape(PAD, -1)

    def combine(y, first):
        for start in (first, first + 256):
            lanes = slice(start, min(start + 256, FLAT))
            y[:, lanes] = jnp.dot(table[...], scaled[:, lanes], preferred_element_type=f32).astype(bf16)

    for step in (0, 1, 2, 3, 4, 6, 5, 7):
        group = group_of(step)
        arrive_planes(*x_planes(group))
        if step:
            a2a_middle(part, group).wait_recv()
        else:
            own_middle.wait()
        scale_group(x1, group)
    combine(y1, 0)
    for group in range(groups):
        start_low(y_planes(group)[0])
    combine(y1, 512)

    for step in range(groups):
        start_high(y_planes(step)[1])

    def row_copy(source, target, index, other, group):
        rows = rows_of(group)
        return pltpu.make_async_remote_copy(
            src_ref=source.at[rows, :], dst_ref=target.at[rows, :],
            send_sem=h_send.at[index * groups + group], recv_sem=h_recv.at[index * groups + group],
            device_id=(other, slab), device_id_type=MESH,
        )

    def rows_left(group):
        return row_copy(edge_high, halo_high, 0, part - 1, group)

    def rows_right(group):
        return row_copy(edge_low, halo_low, 1, part + 1, group)

    for group in range(groups):
        at = pl.ds(group * PAD, PAD)
        tile = [y1[at, t * 128 : t * 128 + 128].astype(f32) for t in range(7)]
        up = [pltpu.roll(tile[t], 32, 1) for t in (0, 4, 2)]
        edge_high[at, 0:128] = jnp.where((tile_lane >= 32) & (tile_lane < 80), up[0], up[1]).astype(bf16)
        edge_high[at, 128:256] = up[2].astype(bf16)
        down = [pltpu.roll(tile[t], 96, 1) for t in (1, 2, 6, 4)]
        edge_low[at, 0:128] = jnp.where(
            tile_lane >= 96, down[1], jnp.where(tile_lane >= 80, down[0], down[2])
        ).astype(bf16)
        edge_low[at, 128:256] = down[3].astype(bf16)
        pl.when(left)(lambda: rows_left(group).start())
        pl.when(right)(lambda: rows_right(group).start())

    def out_copy(y, land, peer, source, sems, lanes=(0, FLAT), shift=0):
        window = pl.ds(lanes[0], lanes[1])
        return pltpu.make_async_remote_copy(
            src_ref=y.at[rows_of(peer), window], dst_ref=land.at[source, :, window],
            send_sem=sems[0].at[shift + peer], recv_sem=sems[1].at[shift + source],
            device_id=(peer, slab), device_id_type=MESH,
        )

    def start_out(y, land, sems, *how):
        for step in (2, 3, 4, 6, 5, 7, 1):
            out_copy(y, land, group_of(step), part, sems, *how).start()

    def leave_out(y, land, sems, *how):
        for step in range(1, groups):
            out_copy(y, land, group_of(step), part, sems, *how).wait_send()

    def arrive_out(y, land, sems, *how):
        for step in range(1, groups):
            out_copy(y, land, part, group_of(step), sems, *how).wait_recv()

    o1_sems, o2_sems = (o1_send, o1_recv), (o2_send, o2_recv)
    def windows(group):
        at = pl.ds(group * PAD, PAD)
        tile = [y1[at, t * 128 : t * 128 + 128].astype(f32) for t in (2, 4, 6)]
        high, high_b = (halo_high[at, t : t + 128].astype(f32) for t in (0, 128))
        low, low_b = (halo_low[at, t : t + 128].astype(f32) for t in (0, 128))
        x2[1, at, 0:256] = y1[at, 0:256]
        x2[1, at, 256:384] = jnp.where(
            tile_lane < 32, tile[0], jnp.where(tile_lane < 80, high, low)
        ).astype(bf16)
        x2[3, at, 0:128] = jnp.where(tile_lane < 32, low_b, tile[0]).astype(bf16)
        x2[3, at, 128:256] = y1[at, 384:512]
        x2[3, at, 256:384] = jnp.where(
            tile_lane < 64, tile[1], jnp.where(tile_lane < 112, high_b, low_b)
        ).astype(bf16)
        x2[2, at, 0:128] = jnp.where(
            tile_lane < 16, high, jnp.where(tile_lane < 64, low, tile[1])
        ).astype(bf16)
        x2[2, at, 128:256] = y1[at, 640:768]
        x2[2, at, 256:384] = jnp.where(tile_lane < 96, tile[2], high).astype(bf16)

    own1 = pltpu.make_async_copy(y1.at[rows_of(part), :], land1.at[part], self_sem)
    for group in range(groups):
        pl.when(left)(lambda: rows_right(group).wait_recv())
        pl.when(right)(lambda: rows_left(group).wait_recv())
        windows(group)
        if group == OUT1:
            start_out(y1, land1, o1_sems)
            own1.start()
        arrive_planes(*y_planes(group))
        scale_group(x2, group)
    begin, end = ((0, 512), 0), ((512, FLAT - 512), groups)
    combine(y2, 0)
    start_out(y2, land2, o2_sems, *begin)
    combine(y2, 512)
    start_out(y2, land2, o2_sems, *end)
    own1.wait()
    own2 = pltpu.make_async_copy(y2.at[rows_of(part), :], land2.at[part], self_sem)
    own2.start()

    def assemble(land, out_ref, planes):
        for plane in planes:
            carry = None
            for source in range(groups):
                tile, offset = divmod(CELLS * source, 128)
                start = 256 * plane
                block = land[source, 0:own_rows, start : start + WIN].astype(f32)
                if offset != 32 * plane:
                    block = pltpu.roll(block, (offset - 32 * plane) % WIN, 1)
                head = block[:, 0:128]
                if offset:
                    head = jnp.where(tile_lane < offset, carry, head)
                out_ref[plane, :, tile * 128 : tile * 128 + 128] = head.astype(bf16)
                out_ref[plane, :, tile * 128 + 128 : tile * 128 + 256] = block[:, 128:256].astype(bf16)
                carry = block[:, 256:384]
                if offset + CELLS == WIN:
                    out_ref[plane, :, tile * 128 + 256 : tile * 128 + 384] = carry.astype(bf16)

    arrive_out(y1, land1, o1_sems)
    assemble(land1, first_ref, range(3))

    leave_planes(*coef_copies)
    for step in range(groups):
        leave_planes(*x_planes(group_of(step)))
        leave_planes(*y_planes(step))
        pl.when(left)(lambda: rows_left(step).wait_send())
        pl.when(right)(lambda: rows_right(step).wait_send())
    for step in range(1, groups):
        a2a(group_of(step), part).wait_send()
        a2a_middle(group_of(step), part).wait_send()
    leave_out(y1, land1, o1_sems)

    own2.wait()
    arrive_out(y2, land2, o2_sems, *begin)
    assemble(land2, second_ref, (0,))
    arrive_out(y2, land2, o2_sems, *end)
    assemble(land2, second_ref, (1, 2))
    for how in (begin, end):
        leave_out(y2, land2, o2_sems, *how)


def shards(groups, slabs, panels, mean_field, fluctuations, products, triples, owner_slot):
    fields, nnz = 1 + fluctuations.shape[0], products.shape[0]
    entries = -(-nnz // 128) * 128
    panel_planes = jnp.transpose(panels, (1, 0, 2))
    vmem = pl.BlockSpec(memory_space=pltpu.VMEM)
    out = jax.ShapeDtypeStruct(panel_planes.shape, jnp.bfloat16)
    bf16, f32 = jnp.bfloat16, jnp.float32
    dma = pltpu.SemaphoreType.DMA
    operands = (panel_planes, mean_field, fluctuations, triples.T, products, owner_slot)
    first, second = pl.pallas_call(
        functools.partial(kernel, groups, slabs, fields, nnz),
        out_shape=(out, out),
        in_specs=[pl.BlockSpec(memory_space=pltpu.HBM)] * 6,
        out_specs=(vmem, vmem),
        scratch_shapes=[
            pltpu.VMEM(panel_planes.shape, bf16),
            pltpu.VMEM(mean_field.shape, f32),
            pltpu.VMEM(fluctuations.shape, f32),
            pltpu.VMEM((3, nnz), jnp.int32),
            pltpu.VMEM((nnz,), f32),
            pltpu.VMEM(owner_slot.shape, jnp.int32),
            dma((6,)),
            pltpu.VMEM((groups, 3, PAD, WIN), bf16),
            pltpu.VMEM((5, ROWS, WIN), bf16),
            pltpu.VMEM((5, ROWS, WIN), bf16),
            pltpu.VMEM((ROWS, FLAT), bf16),
            pltpu.VMEM((ROWS, FLAT), bf16),
            pltpu.VMEM((ROWS, 256), bf16),
            pltpu.VMEM((ROWS, 256), bf16),
            pltpu.VMEM((ROWS, 256), bf16),
            pltpu.VMEM((ROWS, 256), bf16),
            pltpu.VMEM((groups, PAD, FLAT), bf16),
            pltpu.VMEM((groups, PAD, FLAT), bf16),
            pltpu.VMEM((3, 8, WIN), f32),
            pltpu.VMEM((8, WIN), f32),
            pltpu.VMEM((8, WIN), f32),
            pltpu.VMEM((fields, 6, 8, FLAT), bf16),
            pltpu.VMEM((3, 2, 16, WIN), bf16),
            pltpu.VMEM((3 + fields, 16, entries), bf16),
            pltpu.VMEM((6, PAD, FLAT), bf16),
            pltpu.VMEM((2 * ROWS, entries), bf16),
            pltpu.VMEM((ROWS, entries), bf16),
            pltpu.VMEM((ROWS, fields * ROWS), bf16),
            pltpu.VMEM((fields * ROWS, FLAT), bf16),
            dma((groups,)), dma((groups,)), dma((groups,)), dma((groups,)), dma, dma,
            dma((2 * groups,)), dma((2 * groups,)), dma((2,)), dma((2,)), dma((2 * groups,)), dma((2 * groups,)),
            dma((groups,)), dma((groups,)), dma((2 * groups,)), dma((2 * groups,)),
            dma((2 * groups,)), dma((2 * groups,)),
        ],
        compiler_params=pltpu.CompilerParams(
            collective_id=0, has_side_effects=True, vmem_limit_bytes=48 * 1024 * 1024
        ),
    )(*(pltpu.with_memory_space_constraint(operand, pltpu.HBM) for operand in operands))
    return jnp.transpose(first, (1, 0, 2)), jnp.transpose(second, (1, 0, 2))


def solution(mesh):
    in_specs = (P("chaos", "space", None), P("space", None), P(None, "space", None), P(), P(), P())
    out_specs = (P("chaos", "space", None), P("chaos", "space", None))
    body = functools.partial(shards, mesh.shape["chaos"], mesh.shape["space"])
    return jax.shard_map(body, mesh=mesh, in_specs=in_specs, out_specs=out_specs, check_vma=False)
```
